1024 devices in a mesh: ctx: 16 (over x_hi, y), dp: 64 (over z, x_lo, core).
Axes of the slice: x: 4 (x_hi: 2, x_lo: 2; x = x_hi * 2 + x_lo), y: 8, z: 16, core: 2. Of those that a mesh axis runs over, the one named last changes fastest.
Arguments:
- queries: bfloat16 [64, 16384, 128], P('dp', 'ctx'), may hold values from -24 to 24
- keys: bfloat16 [64, 16384, 128], P('dp', 'ctx'), may hold values from -24 to 24
- values: bfloat16 [64, 16384, 128], P('dp', 'ctx'), may hold values from -6 to 6
- grad_out: bfloat16 [64, 16384, 128], P('dp', 'ctx'), may hold values from -6 to 6
- gain: float32 [1024], P('dp'), may hold values from 0.1 to 1.9
- doc_start: int32 [8, 16384], replicated, may hold values from 0 to 16383, as said below
- win_start: int32 [8, 16384], replicated, may hold values from 0 to 16256, as said below
Outputs:
- grad_queries: bfloat16 [64, 16384, 128], P('dp', 'ctx')
- grad_keys: bfloat16 [64, 16384, 128], P('dp', 'ctx')
- grad_values: bfloat16 [64, 16384, 128], P('dp', 'ctx')
- grad_gain: float32 [1024], P('dp')
The draws below stay inside these ranges and needn't reach their ends.
Inputs may be any that keep to these rules, and one draw needn't show every extreme that they name: Documents are contiguous runs of positions: doc_start of a row is at most its position, equals its own position at a document's first row, and is the same for all rows of a document. win_start is a multiple of 128, at most the start of the row's block of 128 positions and at least (7) * 128 positions before that start.
All inputs are finite; a program needn't handle non-finite values.
Results may differ from the reference program's by a relative error of at most 0.012.
The reference program's roundings to bfloat16 on the way (of `scaled`, `attn_probs` and `score_grad`) count: a program that leaves them out, or rounds other values in their place, can miss the bound.
Values may be sent and summed in bfloat16 or wider, within the bound.
A program may use at most 64 MiB of HBM per device.

```python
import math
import jax
import jax.numpy as jnp
from jax import lax

HEADS = 8
HD = 128
BLK = 128
WBLK = 8
TOK_DEV = 1024
BH = 64
SEQS = 8
TOKENS = 16384
N_CTX = 16


def paired_fields(key):
    array_shape = (BH, TOKENS, HD)
    query_base = jnp.clip(jax.random.normal(jax.random.fold_in(key, 101), array_shape, jnp.float32), -6.0, 6.0)
    key_base = jnp.clip(jax.random.normal(jax.random.fold_in(key, 102), array_shape, jnp.float32), -6.0, 6.0)
    return (query_base, key_base)


def draw_queries(key, part):
    return paired_fields(key)[0].astype(jnp.bfloat16)


def draw_keys(key, part):
    return paired_fields(key)[1].astype(jnp.bfloat16)


def bounds_pair(key):
    positions = jnp.arange(TOKENS, dtype=jnp.int32)
    start_flags = jax.random.randint(jax.random.fold_in(key, 201), (SEQS, TOKENS), 0, 700) == 0
    start_flags = start_flags | (positions == 0)[None, :] | (positions == TOKENS - 1)[None, :]
    starts = lax.cummax(jnp.where(start_flags, positions[None, :], 0), axis=1).astype(jnp.int32)
    block_index = positions // BLK
    reach_blocks = jax.random.randint(jax.random.fold_in(key, 202), (SEQS, TOKENS // BLK), 0, WBLK).astype(jnp.int32)
    reach_rows = jnp.repeat(reach_blocks, BLK, axis=1)
    window_floor = jnp.maximum(block_index[None, :] - reach_rows, 0) * BLK
    aligned = starts // BLK * BLK
    window = jnp.maximum(aligned, window_floor)
    return (starts, window.astype(jnp.int32))


def draw_doc_start(key, part):
    return bounds_pair(key)[0]


def draw_win_start(key, part):
    return bounds_pair(key)[1]


def steps_of(own_key, dims, shards, smallest, high):
    def one(axis_at, shards_of):
        steps = jax.random.uniform(jax.random.fold_in(jax.random.fold_in(own_key, 6), axis_at), (shards_of,), jnp.float32, smallest / len(shards), high / len(shards))
        return jnp.repeat(jnp.exp(steps), dims[axis_at] // shards_of).reshape((-1,) + (1,) * (len(dims) - axis_at - 1))

    factor_of = one(*shards[0])
    for cut in shards[1:]:
        factor_of = factor_of * one(*cut)
    return factor_of


def bell_draw(rng, dims, width, most, shards=(), kind=jnp.bfloat16):
    entries = width * jax.random.normal(rng, dims, jnp.float32)
    if shards:
        entries = entries * steps_of(rng, dims, shards, -0.22, 0.18)
    return jnp.clip(entries, -most, most).astype(kind)


def setup_inputs(seed: int = 0) -> dict:
    key_of = jax.random.split(jax.random.key(seed), 8)
    return {
        "queries": draw_queries(jax.random.fold_in(key_of[7], 71), 0),
        "keys": draw_keys(jax.random.fold_in(key_of[7], 71), 0),
        "values": bell_draw(key_of[2], (BH, TOKENS, HD), 1.0, 6.0, ((0, 64), (1, 16))),
        "grad_out": bell_draw(key_of[3], (BH, TOKENS, HD), 1.0, 6.0, ((0, 64), (1, 16))),
        "gain": jnp.clip(1.0 + 0.18 * jax.random.normal(key_of[4], (HEADS * HD,), jnp.float32), 0.1, 1.9),
        "doc_start": draw_doc_start(jax.random.fold_in(key_of[7], 71), 0),
        "win_start": draw_win_start(jax.random.fold_in(key_of[7], 71), 0),
    }


def rounded(array):
    return lax.optimization_barrier(array.astype(jnp.bfloat16)).astype(jnp.float32)

def spread(parts, pair_count, tok_rows, head_width):
    summed = jnp.zeros((pair_count, (WBLK - 1) * BLK + tok_rows, head_width), jnp.float32)
    for offset in range(WBLK):
        slab_rows = parts[:, :, offset * BLK:(offset + 1) * BLK].reshape(pair_count, tok_rows, head_width)
        summed = summed + jnp.pad(slab_rows, ((0, 0), (offset * BLK, (WBLK - 1 - offset) * BLK), (0, 0)))
    return summed

def band_grads(scaled, key_ext, value_ext, grad_rows, lower_bound, first_row):
    pair_count, tok_rows, head_width = scaled.shape
    nblock = tok_rows // BLK
    prev_rows = (WBLK - 1) * BLK
    span_cols = WBLK * BLK
    score_scale = 1.0 / math.sqrt(head_width)
    query_blocks = scaled.astype(jnp.float32).reshape(pair_count, nblock, BLK, head_width)
    grad_blocks = grad_rows.astype(jnp.float32).reshape(pair_count, nblock, BLK, head_width)
    key_window = jnp.concatenate([key_ext[:, offset * BLK:offset * BLK + tok_rows].reshape(pair_count, nblock, BLK, head_width) for offset in range(WBLK)], axis=2).astype(jnp.float32)
    value_window = jnp.concatenate([value_ext[:, offset * BLK:offset * BLK + tok_rows].reshape(pair_count, nblock, BLK, head_width) for offset in range(WBLK)], axis=2).astype(jnp.float32)
    query_pos = (first_row + jnp.arange(tok_rows, dtype=jnp.int32)).reshape(nblock, BLK)
    key_pos = first_row - prev_rows + (jnp.arange(nblock, dtype=jnp.int32) * BLK)[:, None] + jnp.arange(span_cols, dtype=jnp.int32)[None, :]
    visible = (key_pos[:, None, :] >= lower_bound.reshape(nblock, BLK)[:, :, None]) & (key_pos[:, None, :] <= query_pos[:, :, None])
    scores = jnp.einsum('bnqd,bnkd->bnqk', query_blocks, key_window) * score_scale
    scores = jnp.where(visible[None], scores, -jnp.inf)
    weights = jnp.exp(scores - lax.optimization_barrier(jnp.max(scores, axis=-1, keepdims=True)))
    attn_probs = rounded(weights / lax.optimization_barrier(jnp.sum(weights, axis=-1, keepdims=True)))
    prob_grad = jnp.einsum('bnqd,bnkd->bnqk', grad_blocks, value_window)
    row_delta = lax.optimization_barrier(jnp.sum(attn_probs * prob_grad, axis=-1, keepdims=True))
    score_grad = rounded(attn_probs * (prob_grad - row_delta))
    grad_scaled = jnp.einsum('bnqk,bnkd->bnqd', score_grad, key_window) * score_scale
    key_parts = jnp.einsum('bnqk,bnqd->bnkd', score_grad, query_blocks) * score_scale
    value_parts = jnp.einsum('bnqk,bnqd->bnkd', attn_probs, grad_blocks)
    return (grad_scaled.reshape(pair_count, tok_rows, head_width), spread(key_parts, pair_count, tok_rows, head_width), spread(value_parts, pair_count, tok_rows, head_width))

def to_heads(array):
    return array.reshape(SEQS, HEADS, TOKENS, HD)

def reference(queries, keys, values, grad_out, gain, doc_start, win_start):
    prev_rows = (WBLK - 1) * BLK
    gain_rows = gain.reshape(HEADS, HD)

    def one_sequence(inputs):
        seq_query, seq_key, seq_value, seq_grad, seq_doc, seq_win = inputs
        scaled = lax.optimization_barrier((seq_query.astype(jnp.float32) * gain_rows[:, None, :]).astype(jnp.bfloat16))
        lower_bound = jnp.maximum(seq_doc, seq_win)
        pad_zeros = jnp.zeros((HEADS, prev_rows, HD), seq_key.dtype)
        padded_key = jnp.concatenate([pad_zeros, seq_key], axis=1)
        padded_value = jnp.concatenate([pad_zeros, seq_value], axis=1)
        key_total = jnp.zeros((HEADS, prev_rows + TOKENS, HD), jnp.float32)
        value_total = jnp.zeros((HEADS, prev_rows + TOKENS, HD), jnp.float32)
        grad_pieces = []
        for shard_index in range(N_CTX):
            first_row = shard_index * TOK_DEV
            last_row = first_row + TOK_DEV
            grad_scaled, key_grad, value_grad = band_grads(scaled[:, first_row:last_row], padded_key[:, first_row:first_row + prev_rows + TOK_DEV], padded_value[:, first_row:first_row + prev_rows + TOK_DEV], seq_grad[:, first_row:last_row], lower_bound[first_row:last_row], first_row)
            key_total = key_total.at[:, first_row + prev_rows:last_row + prev_rows].add(key_grad[:, prev_rows:])
            key_total = key_total.at[:, first_row:first_row + prev_rows].add(rounded(key_grad[:, :prev_rows]))
            value_total = value_total.at[:, first_row + prev_rows:last_row + prev_rows].add(value_grad[:, prev_rows:])
            value_total = value_total.at[:, first_row:first_row + prev_rows].add(rounded(value_grad[:, :prev_rows]))
            grad_pieces.append(grad_scaled)
        grad_all = jnp.concatenate(grad_pieces, axis=1)
        grad_query = (grad_all * gain_rows[:, None, :]).astype(jnp.bfloat16)
        grad_heads = lax.optimization_barrier(jnp.sum(grad_all * seq_query.astype(jnp.float32), axis=1))
        return (grad_query, key_total[:, prev_rows:].astype(jnp.bfloat16), value_total[:, prev_rows:].astype(jnp.bfloat16), grad_heads)
    grad_query, grad_key, grad_value, grad_heads = lax.map(one_sequence, (to_heads(queries), to_heads(keys), to_heads(values), to_heads(grad_out), doc_start, win_start))
    return (grad_query.reshape(BH, TOKENS, HD), grad_key.reshape(BH, TOKENS, HD), grad_value.reshape(BH, TOKENS, HD), lax.optimization_barrier(jnp.sum(grad_heads, axis=0)).reshape(HEADS * HD))
```

```python
import functools
import math

import jax
import jax.numpy as jnp
from jax import lax
from jax.experimental import pallas as pl
from jax.experimental.pallas import tpu as pltpu
from jax.sharding import PartitionSpec as P

HEADS = 8
BLK = 128
WBLK = 8
HALO = (WBLK - 1) * BLK
STEP = 2 * BLK
PIECE = HALO // 4
MESH = pl.DeviceIdType.MESH
NEG = -1e30


def send(source, target, send_sem, recv_sem, device):
    return pltpu.make_async_remote_copy(
        src_ref=source,
        dst_ref=target,
        send_sem=send_sem,
        recv_sem=recv_sem,
        device_id=device,
        device_id_type=MESH,
    )


def body(
    n_ctx,
    q_hbm, k_hbm, v_hbm, g_hbm, share_ref, doc_hbm, win_hbm,
    dq_ref, dk_ref, dv_ref, gg_ref,
    q_ref, go_ref, k_ext, v_ext, k_t, scaled, doc_ref, win_ref, low_ref,
    s_scr, p_scr, dp_scr, ds_scr, dk_acc, dv_acc,
    dk_out, dv_out, dk_in, dv_in,
    gain_ref, gain_row, gain_in, part_row, part_in, head_row, head_in, part_acc,
    load_sem, halo_send, halo_recv, back_send, back_recv,
    gain_send, gain_recv, part_send, part_recv, head_send, head_recv,
):
    tok = q_ref.shape[0]
    width = q_ref.shape[1]
    groups = tok // STEP
    window = STEP + HALO
    kblocks = window // BLK
    score_scale = 1.0 / math.sqrt(width)
    exp_scale = score_scale * math.log2(math.e)
    c = lax.axis_index("ctx")
    d = lax.axis_index("dp")
    row = d // HEADS
    mine = d % HEADS
    diagonal = row == mine

    barrier = pltpu.get_barrier_semaphore()
    for hop in range(1, n_ctx):
        pl.semaphore_signal(
            barrier, inc=1, device_id={"ctx": (c + hop) % n_ctx}, device_id_type=MESH
        )
    for other in range(HEADS):
        user = row + HEADS * other
        owner = HEADS * mine + other

        @pl.when(user != d)
        def _():
            pl.semaphore_signal(barrier, inc=1, device_id={"dp": user}, device_id_type=MESH)

        @pl.when(owner != d)
        def _():
            pl.semaphore_signal(barrier, inc=1, device_id={"dp": owner}, device_id_type=MESH)

    first_row = pl.multiple_of(c * tok, tok)
    loads = [
        pltpu.make_async_copy(k_hbm, k_ext.at[pl.ds(HALO, tok)], load_sem.at[0]),
        pltpu.make_async_copy(v_hbm, v_ext.at[pl.ds(HALO, tok)], load_sem.at[1]),
        pltpu.make_async_copy(q_hbm, q_ref, load_sem.at[2]),
        pltpu.make_async_copy(g_hbm, go_ref, load_sem.at[3]),
        pltpu.make_async_copy(doc_hbm.at[:, pl.ds(first_row, tok)], doc_ref, load_sem.at[4]),
        pltpu.make_async_copy(win_hbm.at[:, pl.ds(first_row, tok)], win_ref, load_sem.at[5]),
    ]
    gain_ref[...] = jnp.zeros_like(gain_ref)
    for load in loads:
        load.start()

    @pl.when(c == 0)
    def _():
        k_ext[pl.ds(0, HALO)] = jnp.zeros((HALO, width), k_ext.dtype)
        v_ext[pl.ds(0, HALO)] = jnp.zeros((HALO, width), v_ext.dtype)

    dk_acc[...] = jnp.zeros_like(dk_acc)
    dv_acc[...] = jnp.zeros_like(dv_acc)
    part_acc[...] = jnp.zeros_like(part_acc)

    gain_ref[:, 0 : share_ref.shape[1]] = share_ref[...]
    gain_row[...] = pltpu.roll(gain_ref[...], 16 * mine, 1)

    @pl.when(diagonal)
    def _():
        pl.semaphore_wait(barrier, n_ctx - 1 + 2 * (HEADS - 1))

    @pl.when(jnp.logical_not(diagonal))
    def _():
        pl.semaphore_wait(barrier, n_ctx - 1 + 2 * HEADS)

    def gain_copy(target, slot):
        return send(gain_row, gain_in.at[mine], gain_send.at[slot], gain_recv.at[mine], {"dp": target})

    def halo_copy(which, piece, source, target):
        return send(
            source.at[pl.ds(tok - HALO + piece * PIECE, PIECE)],
            target.at[pl.ds(piece * PIECE, PIECE)],
            halo_send.at[which, piece],
            halo_recv.at[which, piece],
            {"ctx": c + 1},
        )

    for other in range(HEADS):
        user = row + HEADS * other

        @pl.when(user != d)
        def _():
            gain_copy(user, other).start()

        @pl.when(user == d)
        def _():
            gain_in[mine] = gain_row[pl.ds(0, 1)]

    @pl.when(c < n_ctx - 1)
    def _():
        for piece in (3, 2, 1, 0):
            halo_copy(0, piece, k_hbm, k_ext).start()
        for piece in (3, 2, 1, 0):
            halo_copy(1, piece, v_hbm, v_ext).start()

    loads[4].wait()
    loads[5].wait()
    low_ref[...] = jnp.maximum(doc_ref[...], win_ref[...]) - (c * tok - HALO)
    loads[0].wait()
    for block in range(WBLK - 1, WBLK - 1 + tok // BLK):
        k_t[:, pl.ds(block * BLK, BLK)] = k_ext[pl.ds(block * BLK, BLK)].T
    loads[1].wait()
    loads[2].wait()
    loads[3].wait()

    for other in range(HEADS):
        owner = HEADS * mine + other

        @pl.when(owner != d)
        def _():
            send(
                gain_row, gain_in.at[other], gain_send.at[0], gain_recv.at[other], {"dp": owner}
            ).wait_recv()

    gain_all = gain_in[0]
    for other in range(1, HEADS):
        gain_all = gain_all + gain_in[other]
    scaled[...] = (q_ref[...].astype(jnp.float32) * gain_all).astype(scaled.dtype)

    seq = row

    def halo_arrives(which, group, source, target):
        @pl.when(c > 0)
        def _():
            halo_copy(which, group, source, target).wait_recv()

    def dot_nt(left, right):
        return lax.dot_general(
            left, right, (((1,), (1,)), ((), ())), preferred_element_type=jnp.float32
        )

    def softmax_step(step, carry):
        group = groups - 1 - step
        base = pl.multiple_of(group * STEP, STEP)
        halo_arrives(0, group, k_hbm, k_ext)
        query = scaled[pl.ds(base, STEP)]
        lower = low_ref[pl.ds(seq, 1), pl.ds(base, STEP)] - base
        highest = jnp.full((8, STEP), NEG, jnp.float32)
        for kb in range(kblocks):
            scores = dot_nt(k_ext[pl.ds(base + kb * BLK, BLK)], query)
            key_row = lax.broadcasted_iota(jnp.int32, (BLK, STEP), 0) + kb * BLK
            seen = key_row >= lower
            if kb >= WBLK - 1:
                seen = seen & (key_row - HALO <= lax.broadcasted_iota(jnp.int32, (BLK, STEP), 1))
            scores = jnp.where(seen, scores, NEG)
            s_scr[pl.ds(kb * BLK, BLK)] = scores
            highest = jnp.maximum(highest, jnp.max(scores.reshape(BLK // 8, 8, STEP), axis=0))
        highest = jnp.max(highest, axis=0, keepdims=True) * exp_scale
        total = jnp.zeros((8, STEP), jnp.float32)
        for kb in range(kblocks):
            weights = jnp.exp2(s_scr[pl.ds(kb * BLK, BLK)] * exp_scale - highest)
            s_scr[pl.ds(kb * BLK, BLK)] = weights
            total = total + jnp.sum(weights.reshape(BLK // 8, 8, STEP), axis=0)
        inverse = 1.0 / jnp.sum(total, axis=0, keepdims=True)
        for kb in range(kblocks):
            probs = (s_scr[pl.ds(kb * BLK, BLK)] * inverse).astype(p_scr.dtype)
            p_scr[group, pl.ds(kb * BLK, BLK)] = probs
        dv_acc[pl.ds(base, window)] += jnp.dot(
            p_scr[group], go_ref[pl.ds(base, STEP)], preferred_element_type=jnp.float32
        )
        return carry

    lax.fori_loop(0, groups, softmax_step, 0)

    back_dv = send(dv_out, dv_in, back_send.at[0], back_recv.at[0], {"ctx": c - 1})
    back_dk = send(dk_out, dk_in, back_send.at[1], back_recv.at[1], {"ctx": c - 1})

    dv_out[...] = dv_acc[pl.ds(0, HALO)].astype(dv_out.dtype)

    @pl.when(c > 0)
    def _():
        back_dv.start()

    for block in range(WBLK - 1):
        k_t[:, pl.ds(block * BLK, BLK)] = k_ext[pl.ds(block * BLK, BLK)].T

    def grad_step(step, carry):
        group = groups - 1 - step
        base = pl.multiple_of(group * STEP, STEP)
        halo_arrives(1, group, v_hbm, v_ext)
        grad = go_ref[pl.ds(base, STEP)]
        delta = jnp.zeros((8, STEP), jnp.float32)
        for kb in range(kblocks):
            prob_grad = dot_nt(v_ext[pl.ds(base + kb * BLK, BLK)], grad)
            dp_scr[pl.ds(kb * BLK, BLK)] = prob_grad
            terms = prob_grad * p_scr[group, pl.ds(kb * BLK, BLK)].astype(jnp.float32)
            delta = delta + jnp.sum(terms.reshape(BLK // 8, 8, STEP), axis=0)
        delta = jnp.sum(delta, axis=0, keepdims=True)
        for kb in range(kblocks):
            probs = p_scr[group, pl.ds(kb * BLK, BLK)].astype(jnp.float32)
            ds_scr[pl.ds(kb * BLK, BLK)] = (
                probs * (dp_scr[pl.ds(kb * BLK, BLK)] - delta)
            ).astype(ds_scr.dtype)
        score_grad = ds_scr[...]
        mixed_t = jnp.dot(
            k_t[:, pl.ds(base, window)], score_grad, preferred_element_type=jnp.float32
        )
        mixed = mixed_t.T * score_scale
        dq_ref[pl.ds(base, STEP)] = (mixed * gain_all).astype(dq_ref.dtype)
        terms = mixed * q_ref[pl.ds(base, STEP)].astype(jnp.float32)
        part_acc[...] += jnp.sum(terms.reshape(STEP // 8, 8, width), axis=0)
        dk_acc[pl.ds(base, window)] += jnp.dot(
            score_grad, scaled[pl.ds(base, STEP)], preferred_element_type=jnp.float32
        )
        return carry

    lax.fori_loop(0, groups, grad_step, 0)

    part_row[...] = jnp.sum(part_acc[...], axis=0, keepdims=True)

    def part_copy(hop):
        return send(
            part_row, part_in.at[hop], part_send.at[hop], part_recv.at[hop], {"ctx": (c + hop) % n_ctx}
        )

    for hop in range(1, n_ctx):
        part_copy(hop).start()
    dk_out[...] = (dk_acc[pl.ds(0, HALO)] * score_scale).astype(dk_out.dtype)

    @pl.when(c > 0)
    def _():
        back_dk.start()

    own_dk = dk_acc[pl.ds(HALO, tok)] * score_scale
    dk_acc[pl.ds(HALO, tok)] = own_dk
    dk_ref[...] = own_dk.astype(dk_ref.dtype)

    for hop in range(1, n_ctx):
        part_copy(hop).wait()
    across = part_row[...]
    for hop in range(1, n_ctx):
        across = across + part_in[hop]
    head_row[...] = across

    def head_copy(target, slot):
        return send(head_row, head_in.at[row], head_send.at[slot], head_recv.at[row], {"dp": target})

    for other in range(HEADS):
        owner = HEADS * mine + other

        @pl.when(owner != d)
        def _():
            head_copy(owner, other).start()

        @pl.when(owner == d)
        def _():
            head_in[row] = head_row[...]

    @pl.when(c < n_ctx - 1)
    def _():
        back_dv.wait_recv()

    dv_ref[...] = dv_acc[pl.ds(HALO, tok)].astype(dv_ref.dtype)

    @pl.when(c < n_ctx - 1)
    def _():
        dv_ref[pl.ds(tok - HALO, HALO)] = (
            dv_acc[pl.ds(tok, HALO)] + dv_in[...].astype(jnp.float32)
        ).astype(dv_ref.dtype)
        back_dk.wait_recv()
        dk_ref[pl.ds(tok - HALO, HALO)] = (
            dk_acc[pl.ds(tok, HALO)] + dk_in[...].astype(jnp.float32)
        ).astype(dk_ref.dtype)

    for other in range(HEADS):
        user = row + HEADS * other

        @pl.when(user != d)
        def _():
            send(
                head_row, head_in.at[other], head_send.at[0], head_recv.at[other], {"dp": user}
            ).wait_recv()

    whole = head_in[0]
    for other in range(1, HEADS):
        whole = whole + head_in[other]
    whole = pltpu.roll(jnp.broadcast_to(whole, (8, width)), (width - 16 * mine) % width, 1)
    gg_ref[...] = whole[0:1, 0 : gg_ref.shape[1]]

    for other in range(HEADS):
        user = row + HEADS * other
        owner = HEADS * mine + other

        @pl.when(user != d)
        def _():
            gain_copy(user, other).wait_send()

        @pl.when(owner != d)
        def _():
            head_copy(owner, other).wait_send()

    @pl.when(c < n_ctx - 1)
    def _():
        for piece in range(4):
            halo_copy(0, piece, k_hbm, k_ext).wait_send()
            halo_copy(1, piece, v_hbm, v_ext).wait_send()

    @pl.when(c > 0)
    def _():
        back_dv.wait_send()
        back_dk.wait_send()


def on_device(queries, keys, values, grad_out, gain, doc_start, win_start):
    _, tok, width = queries.shape
    n_ctx = lax.axis_size("ctx")
    seqs = doc_start.shape[0]
    share = gain.shape[0]
    window = STEP + HALO
    groups = tok // STEP
    wide = (HALO + tok, width)
    hbm = pl.BlockSpec(memory_space=pl.ANY)
    vmem = pl.BlockSpec(memory_space=pltpu.VMEM)
    dma = pltpu.SemaphoreType.DMA


    grads = pl.pallas_call(
        functools.partial(body, n_ctx),
        out_shape=[jax.ShapeDtypeStruct((tok, width), jnp.bfloat16)] * 3
        + [jax.ShapeDtypeStruct((1, share), jnp.float32)],
        in_specs=[hbm] * 4 + [vmem] + [hbm] * 2,
        out_specs=[vmem] * 4,
        scratch_shapes=[
            pltpu.VMEM((tok, width), jnp.bfloat16),
            pltpu.VMEM((tok, width), jnp.bfloat16),
            pltpu.VMEM(wide, jnp.bfloat16),
            pltpu.VMEM(wide, jnp.bfloat16),
            pltpu.VMEM((width, HALO + tok), jnp.bfloat16),
            pltpu.VMEM((tok, width), jnp.bfloat16),
            pltpu.VMEM((seqs, tok), jnp.int32),
            pltpu.VMEM((seqs, tok), jnp.int32),
            pltpu.VMEM((seqs, tok), jnp.int32),
            pltpu.VMEM((window, STEP), jnp.float32),
            pltpu.VMEM((groups, window, STEP), jnp.bfloat16),
            pltpu.VMEM((window, STEP), jnp.float32),
            pltpu.VMEM((window, STEP), jnp.bfloat16),
            pltpu.VMEM(wide, jnp.float32),
            pltpu.VMEM(wide, jnp.float32),
            pltpu.VMEM((HALO, width), jnp.bfloat16),
            pltpu.VMEM((HALO, width), jnp.bfloat16),
            pltpu.VMEM((HALO, width), jnp.bfloat16),
            pltpu.VMEM((HALO, width), jnp.bfloat16),
            pltpu.VMEM((1, width), jnp.float32),
            pltpu.VMEM((1, width), jnp.float32),
            pltpu.VMEM((HEADS, 1, width), jnp.float32),
            pltpu.VMEM((1, width), jnp.float32),
            pltpu.VMEM((n_ctx, 1, width), jnp.float32),
            pltpu.VMEM((1, width), jnp.float32),
            pltpu.VMEM((HEADS, 1, width), jnp.float32),
            pltpu.VMEM((8, width), jnp.float32),
            dma((6,)),
            dma((2, 4)),
            dma((2, 4)),
            dma((2,)),
            dma((2,)),
            dma((HEADS,)),
            dma((HEADS,)),
            dma((n_ctx,)),
            dma((n_ctx,)),
            dma((HEADS,)),
            dma((HEADS,)),
        ],
        compiler_params=pltpu.CompilerParams(
            collective_id=0, has_side_effects=True, vmem_limit_bytes=60 << 20
        ),
    )(
        queries.reshape(tok, width),
        keys.reshape(tok, width),
        values.reshape(tok, width),
        grad_out.reshape(tok, width),
        gain.reshape(1, share),
        doc_start,
        win_start,
    )
    shape = (1, tok, width)
    return (
        grads[0].reshape(shape),
        grads[1].reshape(shape),
        grads[2].reshape(shape),
        grads[3].reshape(share),
    )


def solution(mesh):
    rows = P("dp", "ctx", None)
    return jax.shard_map(
        on_device,
        mesh=mesh,
        in_specs=(rows, rows, rows, rows, P("dp"), P(), P()),
        out_specs=(rows, rows, rows, P("dp")),
        check_vma=False,
    )
```

```python
import functools
import math

import jax
import jax.numpy as jnp
from jax import lax
from jax.experimental import pallas as pl
from jax.experimental.pallas import tpu as pltpu
from jax.sharding import PartitionSpec as P

HEADS = 8
BLK = 128
WBLK = 8
HALO = (WBLK - 1) * BLK
STEP = 2 * BLK
PIECE = HALO // 4
MESH = pl.DeviceIdType.MESH
NEG = -1e30


def send(source, target, send_sem, recv_sem, device):
    return pltpu.make_async_remote_copy(
        src_ref=source,
        dst_ref=target,
        send_sem=send_sem,
        recv_sem=recv_sem,
        device_id=device,
        device_id_type=MESH,
    )


def body(
    n_ctx,
    q_hbm, k_hbm, v_hbm, g_hbm, share_ref, doc_hbm, win_hbm,
    dq_ref, dk_ref, dv_ref, gg_ref,
    q_ref, go_ref, k_ext, v_ext, k_t, scaled, doc_ref, win_ref, low_ref,
    s_scr, p_scr, dp_scr, ds_scr, dk_acc, dv_acc,
    dk_out, dv_out, dk_in, dv_in,
    gain_ref, gain_row, gain_in, gain_full, part_rows, part_in, head_row, head_in, part_acc,
    load_sem, halo_send, halo_recv, back_send, back_recv,
    gain_send, gain_recv, relay_send, relay_recv, part_send, part_recv, head_send, head_recv, met, met_rows,
):
    tok = q_ref.shape[0]
    width = q_ref.shape[1]
    groups = tok // STEP
    window = STEP + HALO
    kblocks = window // BLK
    score_scale = 1.0 / math.sqrt(width)
    exp_scale = score_scale * math.log2(math.e)
    c = lax.axis_index("ctx")
    d = lax.axis_index("dp")
    row = d // HEADS
    mine = d % HEADS
    diagonal = row == mine

    root = HEADS * row + row
    along = n_ctx // 2
    y = c % along
    y_base = c - y
    far_x = (c + along) % n_ctx
    y_peers = [y_base + (y + hop + along) % along for hop in (2, -2, 1, -1)]
    at_end = (y == 0) | (y == along - 1)
    half = HEADS // 2

    def source_of(other):
        near = jnp.where(other < mine, other + 1, mine)
        late = jnp.where(other < half, mine, near)
        early = jnp.where(other < half, mine, jnp.where(other < half + 2, half - 1, 0))
        return jnp.where(mine >= half, late, early)

    source = source_of(row)
    asked = source < row
    feeds = [(source_of(jnp.int32(t)) == row) & (row != t) for t in range(HEADS)]

    barrier = pltpu.get_barrier_semaphore()

    def greet(device):
        pl.semaphore_signal(barrier, inc=1, device_id=device, device_id_type=MESH)

    @pl.when(c > 0)
    def _():
        greet({"ctx": c - 1})

    @pl.when(at_end)
    def _():
        greet({"ctx": y_base + along - 1 - y})

    @pl.when(c < along)
    def _():
        greet({"ctx": far_x})

    @pl.when(diagonal)
    def _():
        for other in range(1, HEADS):
            greet({"dp": HEADS * row + (row + other) % HEADS})

    @pl.when(row < source)
    def _():
        greet({"dp": HEADS * source + mine})

    for t in range(HEADS):

        @pl.when(feeds[t] & (row < t))
        def _():
            greet({"dp": HEADS * t + mine})

    first_row = pl.multiple_of(c * tok, tok)
    loads = [
        pltpu.make_async_copy(k_hbm, k_ext.at[pl.ds(HALO, tok)], load_sem.at[0]),
        pltpu.make_async_copy(v_hbm, v_ext.at[pl.ds(HALO, tok)], load_sem.at[1]),
        pltpu.make_async_copy(q_hbm, q_ref, load_sem.at[2]),
        pltpu.make_async_copy(g_hbm, go_ref, load_sem.at[3]),
        pltpu.make_async_copy(doc_hbm.at[:, pl.ds(first_row, tok)], doc_ref, load_sem.at[4]),
        pltpu.make_async_copy(win_hbm.at[:, pl.ds(first_row, tok)], win_ref, load_sem.at[5]),
    ]
    gain_ref[...] = jnp.zeros_like(gain_ref)
    for load in loads:
        load.start()

    @pl.when(c == 0)
    def _():
        k_ext[pl.ds(0, HALO)] = jnp.zeros((HALO, width), k_ext.dtype)
        v_ext[pl.ds(0, HALO)] = jnp.zeros((HALO, width), v_ext.dtype)

    dk_acc[...] = jnp.zeros_like(dk_acc)
    dv_acc[...] = jnp.zeros_like(dv_acc)
    part_acc[...] = jnp.zeros_like(part_acc)

    gain_ref[:, 0 : share_ref.shape[1]] = share_ref[...]
    gain_row[...] = pltpu.roll(gain_ref[...], 16 * mine, 1)

    terms = [c < n_ctx - 1, at_end, c >= along, jnp.logical_not(diagonal), asked]
    terms += [feeds[t] & (row > t) for t in range(HEADS)]
    pl.semaphore_wait(barrier, sum(jnp.where(term, 1, 0) for term in terms))

    def halo_copy(which, piece, source, target):
        return send(
            source.at[pl.ds(tok - HALO + piece * PIECE, PIECE)],
            target.at[pl.ds(piece * PIECE, PIECE)],
            halo_send.at[which, piece],
            halo_recv.at[which, piece],
            {"ctx": c + 1},
        )

    to_root = send(gain_row, gain_in.at[mine], gain_send.at[0], gain_recv.at[mine], {"dp": root})

    def feed(t):
        return send(
            gain_full, gain_full, relay_send.at[t], relay_recv.at[0], {"dp": HEADS * t + mine}
        )


    @pl.when(c < n_ctx - 1)
    def _():
        for piece in (3, 2, 1, 0):
            halo_copy(0, piece, k_hbm, k_ext).start()
        for piece in (3, 2, 1, 0):
            halo_copy(1, piece, v_hbm, v_ext).start()

    @pl.when(jnp.logical_not(diagonal))
    def _():
        to_root.start()

    @pl.when(asked)
    def _():
        pl.semaphore_signal(
            met_rows.at[row], inc=1, device_id={"dp": HEADS * source + mine}, device_id_type=MESH
        )

    @pl.when(c >= along)
    def _():
        pl.semaphore_signal(met.at[2], inc=1, device_id={"ctx": far_x}, device_id_type=MESH)

    @pl.when(diagonal)
    def _():
        total = gain_row[...]
        for other in range(1, HEADS):
            piece = (row + other) % HEADS
            send(
                gain_row, gain_in.at[piece], gain_send.at[0], gain_recv.at[piece], {"dp": HEADS * row + piece}
            ).wait_recv()
            total = total + gain_in[piece]
        gain_full[...] = total

    @pl.when(jnp.logical_not(diagonal))
    def _():
        feed(0).wait_recv()

    for t in range(HEADS):

        @pl.when(feeds[t] & (row < t))
        def _():
            pl.semaphore_wait(met_rows.at[t], 1)

        @pl.when(feeds[t])
        def _():
            feed(t).start()

    loads[4].wait()
    loads[5].wait()
    low_ref[...] = jnp.maximum(doc_ref[...], win_ref[...]) - (c * tok - HALO)
    loads[0].wait()
    for block in range(WBLK - 1, WBLK - 1 + tok // BLK):
        k_t[:, pl.ds(block * BLK, BLK)] = k_ext[pl.ds(block * BLK, BLK)].T
    loads[1].wait()
    loads[2].wait()
    loads[3].wait()

    gain_all = gain_full[...]
    scaled[...] = (q_ref[...].astype(jnp.float32) * gain_all).astype(scaled.dtype)

    seq = row

    def halo_arrives(which, group, source, target):
        @pl.when(c > 0)
        def _():
            halo_copy(which, group, source, target).wait_recv()

    def dot_nt(left, right):
        return lax.dot_general(
            left, right, (((1,), (1,)), ((), ())), preferred_element_type=jnp.float32
        )

    def chunk(at):
        return pl.ds(at * BLK, BLK)

    def softmax_step(step, carry):
        group = groups - 1 - step
        base = pl.multiple_of(group * STEP, STEP)
        halo_arrives(0, group, k_hbm, k_ext)
        s_scr[...] = dot_nt(k_ext[pl.ds(base, window)], scaled[pl.ds(base, STEP)])
        lower = low_ref[pl.ds(seq, 1), pl.ds(base, STEP)] - base
        key_row = lax.broadcasted_iota(jnp.int32, (BLK, STEP), 0)
        query_row = lax.broadcasted_iota(jnp.int32, (BLK, STEP), 1)
        highest = jnp.full((8, STEP), NEG, jnp.float32)
        for kb in range(kblocks):
            seen = key_row >= lower - kb * BLK
            if kb >= WBLK - 1:
                seen = seen & (key_row <= query_row + (HALO - kb * BLK))
            scores = jnp.where(seen, s_scr[chunk(kb)], NEG)
            s_scr[chunk(kb)] = scores
            highest = jnp.maximum(highest, jnp.max(scores.reshape(BLK // 8, 8, STEP), axis=0))
        highest = jnp.max(highest, axis=0, keepdims=True) * exp_scale
        total = jnp.zeros((8, STEP), jnp.float32)
        for kb in range(kblocks):
            weights = jnp.exp2(s_scr[chunk(kb)] * exp_scale - highest)
            s_scr[chunk(kb)] = weights
            total = total + jnp.sum(weights.reshape(BLK // 8, 8, STEP), axis=0)
        inverse = 1.0 / jnp.sum(total, axis=0, keepdims=True)
        for kb in range(kblocks):
            p_scr[group, chunk(kb)] = (s_scr[chunk(kb)] * inverse).astype(p_scr.dtype)
        return carry

    lax.fori_loop(0, groups, softmax_step, 0)

    pl.semaphore_signal(met.at[0], inc=1, device_id={"ctx": y_peers[2]}, device_id_type=MESH)
    pl.semaphore_signal(met.at[1], inc=1, device_id={"ctx": y_peers[3]}, device_id_type=MESH)
    for block in range(WBLK - 1):
        k_t[:, pl.ds(block * BLK, BLK)] = k_ext[pl.ds(block * BLK, BLK)].T

    def grad_step(step, carry):
        group = groups - 1 - step
        base = pl.multiple_of(group * STEP, STEP)
        halo_arrives(1, group, v_hbm, v_ext)
        dp_scr[...] = dot_nt(v_ext[pl.ds(base, window)], go_ref[pl.ds(base, STEP)])
        delta = jnp.zeros((8, STEP), jnp.float32)
        for kb in range(kblocks):
            terms = dp_scr[chunk(kb)] * p_scr[group, chunk(kb)].astype(jnp.float32)
            delta = delta + jnp.sum(terms.reshape(BLK // 8, 8, STEP), axis=0)
        delta = jnp.sum(delta, axis=0, keepdims=True)
        for kb in range(kblocks):
            probs = p_scr[group, chunk(kb)].astype(jnp.float32)
            ds_scr[group, chunk(kb)] = (probs * (dp_scr[chunk(kb)] - delta)).astype(ds_scr.dtype)
        mixed_t = jnp.dot(
            k_t[:, pl.ds(base, window)], ds_scr[group], preferred_element_type=jnp.float32
        )
        mixed = mixed_t.T * score_scale
        dq_ref[pl.ds(base, STEP)] = (mixed * gain_all).astype(dq_ref.dtype)
        terms = mixed * q_ref[pl.ds(base, STEP)].astype(jnp.float32)
        part_acc[...] += jnp.sum(terms.reshape(STEP // 8, 8, width), axis=0)
        return carry

    lax.fori_loop(0, groups, grad_step, 0)

    back_dv = send(dv_out, dv_in, back_send.at[0], back_recv.at[0], {"ctx": c - 1})
    back_dk = send(dk_out, dk_in, back_send.at[1], back_recv.at[1], {"ctx": c - 1})

    def key_grads():
        def step(group, carry):
            base = pl.multiple_of(group * STEP, STEP)
            dk_acc[pl.ds(base, window)] += jnp.dot(
                ds_scr[group], scaled[pl.ds(base, STEP)], preferred_element_type=jnp.float32
            )
            return carry

        lax.fori_loop(0, groups, step, 0)
        dk_out[...] = (dk_acc[pl.ds(0, HALO)] * score_scale).astype(dk_out.dtype)

        @pl.when(c > 0)
        def _():
            back_dk.start()

    def value_grads():
        def step(group, carry):
            base = pl.multiple_of(group * STEP, STEP)
            dv_acc[pl.ds(base, window)] += jnp.dot(
                p_scr[group], go_ref[pl.ds(base, STEP)], preferred_element_type=jnp.float32
            )
            return carry

        lax.fori_loop(0, groups, step, 0)
        dv_out[...] = dv_acc[pl.ds(0, HALO)].astype(dv_out.dtype)

        @pl.when(c > 0)
        def _():
            back_dv.start()

    part_rows[0] = jnp.sum(part_acc[...], axis=0, keepdims=True)

    def part_copy(source, slot, target):
        return send(source, part_in.at[slot], part_send.at[slot], part_recv.at[slot], {"ctx": target})

    over_x = part_copy(part_rows.at[0], 0, far_x)
    over_y = [
        part_copy(part_rows.at[1], 1 + at, peer) for at, peer in enumerate(y_peers)
    ]
    on_up = part_copy(part_in.at[3], 5, y_peers[0])
    on_down = part_copy(part_rows.at[2], 6, y_peers[1])

    @pl.when(c < along)
    def _():
        pl.semaphore_wait(met.at[2], 1)

    over_x.start()
    value_grads()
    pl.semaphore_wait(met.at[0], 1)
    pl.semaphore_wait(met.at[1], 1)
    over_x.wait_recv()
    part_rows[1] = part_rows[0] + part_in[0]
    for copy in over_y:
        copy.start()
    key_grads()
    own_dk = dk_acc[pl.ds(HALO, tok)] * score_scale
    dk_acc[pl.ds(HALO, tok)] = own_dk
    dk_ref[...] = own_dk.astype(dk_ref.dtype)
    dv_ref[...] = dv_acc[pl.ds(HALO, tok)].astype(dv_ref.dtype)
    over_y[2].wait_recv()
    on_up.start()
    over_y[1].wait_recv()
    over_y[3].wait_recv()
    part_rows[2] = part_in[2] + part_in[4]
    on_down.start()
    over_y[0].wait_recv()
    across = part_rows[1] + part_in[1] + part_in[2] + part_in[3] + part_in[4]
    on_up.wait_recv()
    on_down.wait_recv()
    head_row[...] = across + part_in[5] + part_in[6]

    def head_copy(target, slot):
        return send(head_row, head_in.at[row], head_send.at[slot], head_recv.at[row], {"dp": target})

    for other in range(HEADS):
        owner = HEADS * mine + other

        @pl.when(owner != d)
        def _():
            head_copy(owner, other).start()

        @pl.when(owner == d)
        def _():
            head_in[row] = head_row[...]

    @pl.when(c < n_ctx - 1)
    def _():
        back_dv.wait_recv()

    @pl.when(c < n_ctx - 1)
    def _():
        dv_ref[pl.ds(tok - HALO, HALO)] = (
            dv_acc[pl.ds(tok, HALO)] + dv_in[...].astype(jnp.float32)
        ).astype(dv_ref.dtype)
        back_dk.wait_recv()
        dk_ref[pl.ds(tok - HALO, HALO)] = (
            dk_acc[pl.ds(tok, HALO)] + dk_in[...].astype(jnp.float32)
        ).astype(dk_ref.dtype)

    for other in range(HEADS):
        user = row + HEADS * other

        @pl.when(user != d)
        def _():
            send(
                head_row, head_in.at[other], head_send.at[0], head_recv.at[other], {"dp": user}
            ).wait_recv()

    whole = head_in[0]
    for other in range(1, HEADS):
        whole = whole + head_in[other]
    whole = pltpu.roll(jnp.broadcast_to(whole, (8, width)), (width - 16 * mine) % width, 1)
    gg_ref[...] = whole[0:1, 0 : gg_ref.shape[1]]

    for other in range(HEADS):
        owner = HEADS * mine + other

        @pl.when(owner != d)
        def _():
            head_copy(owner, other).wait_send()

    for copy in [over_x, *over_y, on_up, on_down]:
        copy.wait_send()

    @pl.when(jnp.logical_not(diagonal))
    def _():
        to_root.wait_send()

    for t in range(HEADS):

        @pl.when(feeds[t])
        def _():
            feed(t).wait_send()

    @pl.when(c < n_ctx - 1)
    def _():
        for piece in range(4):
            halo_copy(0, piece, k_hbm, k_ext).wait_send()
            halo_copy(1, piece, v_hbm, v_ext).wait_send()

    @pl.when(c > 0)
    def _():
        back_dv.wait_send()
        back_dk.wait_send()


def deliver(*refs):
    sources, targets, held, sems = refs[:4], refs[4:8], refs[8:12], refs[12]
    loads = [
        pltpu.make_async_copy(source, hold, sems.at[0, at])
        for at, (source, hold) in enumerate(zip(sources, held))
    ]
    stores = [
        pltpu.make_async_copy(hold, target, sems.at[1, at])
        for at, (target, hold) in enumerate(zip(targets, held))
    ]
    for load in loads:
        load.start()
    for load, store in zip(loads, stores):
        load.wait()
        store.start()
    for store in stores:
        store.wait()


def on_device(queries, keys, values, grad_out, gain, doc_start, win_start):
    _, tok, width = queries.shape
    n_ctx = lax.axis_size("ctx")
    seqs = doc_start.shape[0]
    share = gain.shape[0]
    window = STEP + HALO
    groups = tok // STEP
    wide = (HALO + tok, width)
    hbm = pl.BlockSpec(memory_space=pl.ANY)
    vmem = pl.BlockSpec(memory_space=pltpu.VMEM)
    dma = pltpu.SemaphoreType.DMA


    grads = pl.pallas_call(
        functools.partial(body, n_ctx),
        out_shape=[jax.ShapeDtypeStruct((tok, width), jnp.bfloat16)] * 3
        + [jax.ShapeDtypeStruct((1, share), jnp.float32)],
        in_specs=[hbm] * 4 + [vmem] + [hbm] * 2,
        out_specs=[vmem] * 4,
        scratch_shapes=[
            pltpu.VMEM((tok, width), jnp.bfloat16),
            pltpu.VMEM((tok, width), jnp.bfloat16),
            pltpu.VMEM(wide, jnp.bfloat16),
            pltpu.VMEM(wide, jnp.bfloat16),
            pltpu.VMEM((width, HALO + tok), jnp.bfloat16),
            pltpu.VMEM((tok, width), jnp.bfloat16),
            pltpu.VMEM((seqs, tok), jnp.int32),
            pltpu.VMEM((seqs, tok), jnp.int32),
            pltpu.VMEM((seqs, tok), jnp.int32),
            pltpu.VMEM((window, STEP), jnp.float32),
            pltpu.VMEM((groups, window, STEP), jnp.bfloat16),
            pltpu.VMEM((window, STEP), jnp.float32),
            pltpu.VMEM((groups, window, STEP), jnp.bfloat16),
            pltpu.VMEM(wide, jnp.float32),
            pltpu.VMEM(wide, jnp.float32),
            pltpu.VMEM((HALO, width), jnp.bfloat16),
            pltpu.VMEM((HALO, width), jnp.bfloat16),
            pltpu.VMEM((HALO, width), jnp.bfloat16),
            pltpu.VMEM((HALO, width), jnp.bfloat16),
            pltpu.VMEM((1, width), jnp.float32),
            pltpu.VMEM((1, width), jnp.float32),
            pltpu.VMEM((HEADS, 1, width), jnp.float32),
            pltpu.VMEM((1, width), jnp.float32),
            pltpu.VMEM((3, 1, width), jnp.float32),
            pltpu.VMEM((7, 1, width), jnp.float32),
            pltpu.VMEM((1, width), jnp.float32),
            pltpu.VMEM((HEADS, 1, width), jnp.float32),
            pltpu.VMEM((8, width), jnp.float32),
            dma((6,)),
            dma((2, 4)),
            dma((2, 4)),
            dma((2,)),
            dma((2,)),
            dma((1,)),
            dma((HEADS,)),
            dma((HEADS,)),
            dma((1,)),
            dma((7,)),
            dma((7,)),
            dma((HEADS,)),
            dma((HEADS,)),
            pltpu.SemaphoreType.REGULAR((3,)),
            pltpu.SemaphoreType.REGULAR((HEADS,)),
        ],
        compiler_params=pltpu.CompilerParams(
            collective_id=0, has_side_effects=True, vmem_limit_bytes=60 << 20
        ),
    )(
        queries.reshape(tok, width),
        keys.reshape(tok, width),
        values.reshape(tok, width),
        grad_out.reshape(tok, width),
        gain.reshape(1, share),
        doc_start,
        win_start,
    )
    grads = pl.pallas_call(
        deliver,
        out_shape=[jax.ShapeDtypeStruct(grad.shape, grad.dtype) for grad in grads],
        in_specs=[hbm] * 4,
        out_specs=[hbm] * 4,
        scratch_shapes=[pltpu.VMEM(grad.shape, grad.dtype) for grad in grads] + [dma((2, 4))],
        compiler_params=pltpu.CompilerParams(vmem_limit_bytes=60 << 20),
    )(*grads)
    shape = (1, tok, width)
    return (
        grads[0].reshape(shape),
        grads[1].reshape(shape),
        grads[2].reshape(shape),
        grads[3].reshape(share),
    )


def solution(mesh):
    rows = P("dp", "ctx", None)
    return jax.shard_map(
        on_device,
        mesh=mesh,
        in_specs=(rows, rows, rows, rows, P("dp"), P(), P()),
        out_specs=(rows, rows, rows, P("dp")),
        check_vma=False,
    )
```

```python
import functools
import math

import jax
import jax.numpy as jnp
from jax import lax
from jax.experimental import pallas as pl
from jax.experimental.pallas import tpu as pltpu
from jax.sharding import PartitionSpec as P

HEADS = 8
BLK = 128
WBLK = 8
HALO = (WBLK - 1) * BLK
STEP = 2 * BLK
PIECE = HALO // 4
MESH = pl.DeviceIdType.MESH
NEG = -1e30


def send(source, target, send_sem, recv_sem, device):
    return pltpu.make_async_remote_copy(
        src_ref=source,
        dst_ref=target,
        send_sem=send_sem,
        recv_sem=recv_sem,
        device_id=device,
        device_id_type=MESH,
    )


def body(
    n_ctx,
    q_hbm, k_hbm, v_hbm, g_hbm, share_ref, doc_hbm, win_hbm,
    dq_ref, dk_ref, dv_ref, gg_ref,
    q_ref, go_ref, k_ext, v_ext, k_t, scaled, doc_ref, win_ref, low_ref,
    s_scr, p_scr, dp_scr, ds_scr, dk_acc, dv_acc,
    dk_out, dv_out, dk_in, dv_in,
    gain_ref, gain_row, gain_in, gain_full, part_rows, part_in, head_row, head_in, part_acc,
    load_sem, halo_send, halo_recv, back_send, back_recv,
    gain_send, gain_recv, relay_send, relay_recv, part_send, part_recv, head_send, head_recv, met, met_rows,
):
    tok = q_ref.shape[0]
    width = q_ref.shape[1]
    groups = tok // STEP
    window = STEP + HALO
    kblocks = window // BLK
    score_scale = 1.0 / math.sqrt(width)
    exp_scale = score_scale * math.log2(math.e)
    c = lax.axis_index("ctx")
    d = lax.axis_index("dp")
    row = d // HEADS
    mine = d % HEADS
    diagonal = row == mine

    root = HEADS * row + row
    along = n_ctx // 2
    y = c % along
    y_base = c - y
    far_x = (c + along) % n_ctx
    y_peers = [y_base + (y + hop + along) % along for hop in (2, -2, 1, -1)]
    at_end = (y == 0) | (y == along - 1)
    half = HEADS // 2

    def source_of(other):
        near = jnp.where(other < mine, other + 1, mine)
        late = jnp.where(other < half, mine, near)
        early = jnp.where(other < half, mine, jnp.where(other < half + 2, half - 1, 0))
        return jnp.where(mine >= half, late, early)

    source = source_of(row)
    asked = source < row
    feeds = [(source_of(jnp.int32(t)) == row) & (row != t) for t in range(HEADS)]

    barrier = pltpu.get_barrier_semaphore()

    def greet(device):
        pl.semaphore_signal(barrier, inc=1, device_id=device, device_id_type=MESH)

    @pl.when(c > 0)
    def _():
        greet({"ctx": c - 1})

    @pl.when(at_end)
    def _():
        greet({"ctx": y_base + along - 1 - y})

    @pl.when(c < along)
    def _():
        greet({"ctx": far_x})

    @pl.when(diagonal)
    def _():
        for other in range(1, HEADS):
            greet({"dp": HEADS * row + (row + other) % HEADS})

    @pl.when(row < source)
    def _():
        greet({"dp": HEADS * source + mine})

    for t in range(HEADS):

        @pl.when(feeds[t] & (row < t))
        def _():
            greet({"dp": HEADS * t + mine})

    first_row = pl.multiple_of(c * tok, tok)
    loads = [
        pltpu.make_async_copy(k_hbm, k_ext.at[pl.ds(HALO, tok)], load_sem.at[0]),
        pltpu.make_async_copy(v_hbm, v_ext.at[pl.ds(HALO, tok)], load_sem.at[1]),
        pltpu.make_async_copy(q_hbm, q_ref, load_sem.at[2]),
        pltpu.make_async_copy(g_hbm, go_ref, load_sem.at[3]),
        pltpu.make_async_copy(doc_hbm.at[:, pl.ds(first_row, tok)], doc_ref, load_sem.at[4]),
        pltpu.make_async_copy(win_hbm.at[:, pl.ds(first_row, tok)], win_ref, load_sem.at[5]),
    ]
    gain_ref[...] = jnp.zeros_like(gain_ref)
    for load in loads:
        load.start()

    @pl.when(c == 0)
    def _():
        k_ext[pl.ds(0, HALO)] = jnp.zeros((HALO, width), k_ext.dtype)
        v_ext[pl.ds(0, HALO)] = jnp.zeros((HALO, width), v_ext.dtype)

    dk_acc[...] = jnp.zeros_like(dk_acc)
    dv_acc[...] = jnp.zeros_like(dv_acc)
    part_acc[...] = jnp.zeros_like(part_acc)

    gain_ref[:, 0 : share_ref.shape[1]] = share_ref[...]
    gain_row[...] = pltpu.roll(gain_ref[...], 16 * mine, 1)

    terms = [c < n_ctx - 1, at_end, c >= along, jnp.logical_not(diagonal), asked]
    terms += [feeds[t] & (row > t) for t in range(HEADS)]
    pl.semaphore_wait(barrier, sum(jnp.where(term, 1, 0) for term in terms))

    def halo_copy(which, piece, source, target):
        return send(
            source.at[pl.ds(tok - HALO + piece * PIECE, PIECE)],
            target.at[pl.ds(piece * PIECE, PIECE)],
            halo_send.at[which, piece],
            halo_recv.at[which, piece],
            {"ctx": c + 1},
        )

    to_root = send(gain_row, gain_in.at[mine], gain_send.at[0], gain_recv.at[mine], {"dp": root})

    def feed(t):
        return send(
            gain_full, gain_full, relay_send.at[t], relay_recv.at[0], {"dp": HEADS * t + mine}
        )


    @pl.when(jnp.logical_not(diagonal))
    def _():
        to_root.start()

    @pl.when(asked)
    def _():
        pl.semaphore_signal(
            met_rows.at[row], inc=1, device_id={"dp": HEADS * source + mine}, device_id_type=MESH
        )

    @pl.when(c >= along)
    def _():
        pl.semaphore_signal(met.at[2], inc=1, device_id={"ctx": far_x}, device_id_type=MESH)

    @pl.when(c < n_ctx - 1)
    def _():
        for piece in (3, 2, 1, 0):
            halo_copy(0, piece, k_hbm, k_ext).start()
        for piece in (3, 2, 1, 0):
            halo_copy(1, piece, v_hbm, v_ext).start()

    hands_on = sum(jnp.where(feed_t, 1, 0) for feed_t in feeds) > 0

    @pl.when(diagonal)
    def _():
        total = gain_row[...]
        for other in range(1, HEADS):
            piece = (row + other) % HEADS
            send(
                gain_row, gain_in.at[piece], gain_send.at[0], gain_recv.at[piece], {"dp": HEADS * row + piece}
            ).wait_recv()
            total = total + gain_in[piece]
        gain_full[...] = total

    @pl.when(jnp.logical_not(diagonal) & hands_on)
    def _():
        feed(0).wait_recv()

    for t in range(HEADS):

        @pl.when(feeds[t] & (row < t))
        def _():
            pl.semaphore_wait(met_rows.at[t], 1)

        @pl.when(feeds[t])
        def _():
            feed(t).start()

    loads[4].wait()
    loads[5].wait()
    low_ref[...] = jnp.maximum(doc_ref[...], win_ref[...]) - (c * tok - HALO)
    loads[0].wait()
    for block in range(WBLK - 1, WBLK - 1 + tok // BLK):
        k_t[:, pl.ds(block * BLK, BLK)] = k_ext[pl.ds(block * BLK, BLK)].T
    loads[1].wait()
    loads[2].wait()
    loads[3].wait()


    seq = row

    def halo_arrives(which, group, source, target):
        @pl.when(c > 0)
        def _():
            halo_copy(which, group, source, target).wait_recv()

    def dot_nt(left, right):
        return lax.dot_general(
            left, right, (((1,), (1,)), ((), ())), preferred_element_type=jnp.float32
        )

    def chunk(at):
        return pl.ds(at * BLK, BLK)

    def chunk(at):
        return pl.ds(at * BLK, BLK)

    @pl.when(c > 0)
    def _():
        for piece in range(4):
            halo_copy(0, piece, k_hbm, k_ext).wait_recv()

    pl.semaphore_signal(met.at[0], inc=1, device_id={"ctx": y_peers[2]}, device_id_type=MESH)
    pl.semaphore_signal(met.at[1], inc=1, device_id={"ctx": y_peers[3]}, device_id_type=MESH)
    for block in range(WBLK - 1):
        k_t[:, pl.ds(block * BLK, BLK)] = k_ext[pl.ds(block * BLK, BLK)].T

    def prob_grad_step(step, carry):
        group = groups - 1 - step
        base = pl.multiple_of(group * STEP, STEP)
        halo_arrives(1, group, v_hbm, v_ext)
        dp_scr[group] = dot_nt(v_ext[pl.ds(base, window)], go_ref[pl.ds(base, STEP)])
        return carry

    lax.fori_loop(0, groups, prob_grad_step, 0)

    pl.semaphore_wait(met.at[0], 1)
    pl.semaphore_wait(met.at[1], 1)

    @pl.when(c < along)
    def _():
        pl.semaphore_wait(met.at[2], 1)

    pl.semaphore_signal(met.at[3], inc=1, device_id={"ctx": far_x}, device_id_type=MESH)

    @pl.when(jnp.logical_not(diagonal | hands_on))
    def _():
        feed(0).wait_recv()

    gain_all = gain_full[...]
    scaled[...] = (q_ref[...].astype(jnp.float32) * gain_all).astype(scaled.dtype)

    def query_step(step, carry):
        group = groups - 1 - step
        base = pl.multiple_of(group * STEP, STEP)
        s_scr[...] = dot_nt(k_ext[pl.ds(base, window)], scaled[pl.ds(base, STEP)])
        lower = low_ref[pl.ds(seq, 1), pl.ds(base, STEP)] - base
        key_row = lax.broadcasted_iota(jnp.int32, (BLK, STEP), 0)
        query_row = lax.broadcasted_iota(jnp.int32, (BLK, STEP), 1)
        highest = jnp.full((8, STEP), NEG, jnp.float32)
        for kb in range(kblocks):
            seen = key_row >= lower - kb * BLK
            if kb >= WBLK - 1:
                seen = seen & (key_row <= query_row + (HALO - kb * BLK))
            scores = jnp.where(seen, s_scr[chunk(kb)], NEG)
            s_scr[chunk(kb)] = scores
            highest = jnp.maximum(highest, jnp.max(scores.reshape(BLK // 8, 8, STEP), axis=0))
        highest = jnp.max(highest, axis=0, keepdims=True) * exp_scale
        total = jnp.zeros((8, STEP), jnp.float32)
        for kb in range(kblocks):
            weights = jnp.exp2(s_scr[chunk(kb)] * exp_scale - highest)
            s_scr[chunk(kb)] = weights
            total = total + jnp.sum(weights.reshape(BLK // 8, 8, STEP), axis=0)
        inverse = 1.0 / jnp.sum(total, axis=0, keepdims=True)
        delta = jnp.zeros((8, STEP), jnp.float32)
        for kb in range(kblocks):
            probs = (s_scr[chunk(kb)] * inverse).astype(p_scr.dtype)
            p_scr[group, chunk(kb)] = probs
            products = dp_scr[group, chunk(kb)] * probs.astype(jnp.float32)
            delta = delta + jnp.sum(products.reshape(BLK // 8, 8, STEP), axis=0)
        delta = jnp.sum(delta, axis=0, keepdims=True)
        for kb in range(kblocks):
            probs = p_scr[group, chunk(kb)].astype(jnp.float32)
            ds_scr[group, chunk(kb)] = (probs * (dp_scr[group, chunk(kb)] - delta)).astype(
                ds_scr.dtype
            )
        mixed_t = jnp.dot(
            k_t[:, pl.ds(base, window)], ds_scr[group], preferred_element_type=jnp.float32
        )
        mixed = mixed_t.T * score_scale
        dq_ref[pl.ds(base, STEP)] = (mixed * gain_all).astype(dq_ref.dtype)
        products = mixed * q_ref[pl.ds(base, STEP)].astype(jnp.float32)
        part_acc[...] += jnp.sum(products.reshape(STEP // 8, 8, width), axis=0)
        return carry

    lax.fori_loop(0, groups, query_step, 0, unroll=True)

    back_dv = send(dv_out, dv_in, back_send.at[0], back_recv.at[0], {"ctx": c - 1})
    back_dk = send(dk_out, dk_in, back_send.at[1], back_recv.at[1], {"ctx": c - 1})

    def key_grads():
        def step(group, carry):
            base = pl.multiple_of(group * STEP, STEP)
            dk_acc[pl.ds(base, window)] += jnp.dot(
                ds_scr[group], scaled[pl.ds(base, STEP)], preferred_element_type=jnp.float32
            )
            return carry

        lax.fori_loop(0, groups, step, 0)
        dk_out[...] = (dk_acc[pl.ds(0, HALO)] * score_scale).astype(dk_out.dtype)

        @pl.when(c > 0)
        def _():
            back_dk.start()

    def value_grads():
        def step(group, carry):
            base = pl.multiple_of(group * STEP, STEP)
            dv_acc[pl.ds(base, window)] += jnp.dot(
                p_scr[group], go_ref[pl.ds(base, STEP)], preferred_element_type=jnp.float32
            )
            return carry

        lax.fori_loop(0, groups, step, 0)
        dv_out[...] = dv_acc[pl.ds(0, HALO)].astype(dv_out.dtype)

        @pl.when(c > 0)
        def _():
            back_dv.start()

    part_rows[0] = jnp.sum(part_acc[...], axis=0, keepdims=True)

    def part_copy(source, slot, target):
        return send(source, part_in.at[slot], part_send.at[slot], part_recv.at[slot], {"ctx": target})

    x_peers = [(peer + along) % n_ctx for peer in y_peers]
    targets = x_peers + y_peers + [far_x]
    spread = [part_copy(part_rows.at[0], at, target) for at, target in enumerate(targets)]
    on_up = part_copy(part_rows.at[1], 9, y_peers[0])
    on_down = part_copy(part_rows.at[2], 10, y_peers[1])
    pl.semaphore_wait(met.at[3], 1)
    for copy in spread:
        copy.start()
    value_grads()
    key_grads()
    spread[2].wait_recv()
    spread[6].wait_recv()
    part_rows[1] = part_in[2] + part_in[6]
    on_up.start()
    for at in (1, 3, 5, 7):
        spread[at].wait_recv()
    part_rows[2] = part_in[1] + part_in[3] + part_in[5] + part_in[7]
    on_down.start()
    own_dk = dk_acc[pl.ds(HALO, tok)] * score_scale
    dk_acc[pl.ds(HALO, tok)] = own_dk
    dk_ref[...] = own_dk.astype(dk_ref.dtype)
    dv_ref[...] = dv_acc[pl.ds(HALO, tok)].astype(dv_ref.dtype)
    for at in (0, 4, 8):
        spread[at].wait_recv()
    across = part_rows[0] + part_in[8] + part_rows[1] + part_rows[2] + part_in[0] + part_in[4]
    on_up.wait_recv()
    on_down.wait_recv()
    head_row[...] = across + part_in[9] + part_in[10]

    def head_copy(target, slot):
        return send(head_row, head_in.at[row], head_send.at[slot], head_recv.at[row], {"dp": target})

    for other in range(HEADS):
        owner = HEADS * mine + other

        @pl.when(owner != d)
        def _():
            head_copy(owner, other).start()

        @pl.when(owner == d)
        def _():
            head_in[row] = head_row[...]

    @pl.when(c < n_ctx - 1)
    def _():
        back_dv.wait_recv()

    @pl.when(c < n_ctx - 1)
    def _():
        dv_ref[pl.ds(tok - HALO, HALO)] = (
            dv_acc[pl.ds(tok, HALO)] + dv_in[...].astype(jnp.float32)
        ).astype(dv_ref.dtype)
        back_dk.wait_recv()
        dk_ref[pl.ds(tok - HALO, HALO)] = (
            dk_acc[pl.ds(tok, HALO)] + dk_in[...].astype(jnp.float32)
        ).astype(dk_ref.dtype)

    for other in range(HEADS):
        user = row + HEADS * other

        @pl.when(user != d)
        def _():
            send(
                head_row, head_in.at[other], head_send.at[0], head_recv.at[other], {"dp": user}
            ).wait_recv()

    whole = head_in[0]
    for other in range(1, HEADS):
        whole = whole + head_in[other]
    whole = pltpu.roll(jnp.broadcast_to(whole, (8, width)), (width - 16 * mine) % width, 1)
    gg_ref[...] = whole[0:1, 0 : gg_ref.shape[1]]

    for other in range(HEADS):
        owner = HEADS * mine + other

        @pl.when(owner != d)
        def _():
            head_copy(owner, other).wait_send()

    for copy in [*spread, on_up, on_down]:
        copy.wait_send()

    @pl.when(jnp.logical_not(diagonal))
    def _():
        to_root.wait_send()

    for t in range(HEADS):

        @pl.when(feeds[t])
        def _():
            feed(t).wait_send()

    @pl.when(c < n_ctx - 1)
    def _():
        for piece in range(4):
            halo_copy(0, piece, k_hbm, k_ext).wait_send()
            halo_copy(1, piece, v_hbm, v_ext).wait_send()

    @pl.when(c > 0)
    def _():
        back_dv.wait_send()
        back_dk.wait_send()


def deliver(*refs):
    sources, targets, held, sems = refs[:4], refs[4:8], refs[8:12], refs[12]
    loads = [
        pltpu.make_async_copy(source, hold, sems.at[0, at])
        for at, (source, hold) in enumerate(zip(sources, held))
    ]
    stores = [
        pltpu.make_async_copy(hold, target, sems.at[1, at])
        for at, (target, hold) in enumerate(zip(targets, held))
    ]
    for load in loads:
        load.start()
    for load, store in zip(loads, stores):
        load.wait()
        store.start()
    for store in stores:
        store.wait()


def on_device(queries, keys, values, grad_out, gain, doc_start, win_start):
    _, tok, width = queries.shape
    n_ctx = lax.axis_size("ctx")
    seqs = doc_start.shape[0]
    share = gain.shape[0]
    window = STEP + HALO
    groups = tok // STEP
    wide = (HALO + tok, width)
    hbm = pl.BlockSpec(memory_space=pl.ANY)
    vmem = pl.BlockSpec(memory_space=pltpu.VMEM)
    dma = pltpu.SemaphoreType.DMA


    grads = pl.pallas_call(
        functools.partial(body, n_ctx),
        out_shape=[jax.ShapeDtypeStruct((tok, width), jnp.bfloat16)] * 3
        + [jax.ShapeDtypeStruct((1, share), jnp.float32)],
        in_specs=[hbm] * 4 + [vmem] + [hbm] * 2,
        out_specs=[vmem] * 4,
        scratch_shapes=[
            pltpu.VMEM((tok, width), jnp.bfloat16),
            pltpu.VMEM((tok, width), jnp.bfloat16),
            pltpu.VMEM(wide, jnp.bfloat16),
            pltpu.VMEM(wide, jnp.bfloat16),
            pltpu.VMEM((width, HALO + tok), jnp.bfloat16),
            pltpu.VMEM((tok, width), jnp.bfloat16),
            pltpu.VMEM((seqs, tok), jnp.int32),
            pltpu.VMEM((seqs, tok), jnp.int32),
            pltpu.VMEM((seqs, tok), jnp.int32),
            pltpu.VMEM((window, STEP), jnp.float32),
            pltpu.VMEM((groups, window, STEP), jnp.bfloat16),
            pltpu.VMEM((groups, window, STEP), jnp.float32),
            pltpu.VMEM((groups, window, STEP), jnp.bfloat16),
            pltpu.VMEM(wide, jnp.float32),
            pltpu.VMEM(wide, jnp.float32),
            pltpu.VMEM((HALO, width), jnp.bfloat16),
            pltpu.VMEM((HALO, width), jnp.bfloat16),
            pltpu.VMEM((HALO, width), jnp.bfloat16),
            pltpu.VMEM((HALO, width), jnp.bfloat16),
            pltpu.VMEM((1, width), jnp.float32),
            pltpu.VMEM((1, width), jnp.float32),
            pltpu.VMEM((HEADS, 1, width), jnp.float32),
            pltpu.VMEM((1, width), jnp.float32),
            pltpu.VMEM((3, 1, width), jnp.float32),
            pltpu.VMEM((11, 1, width), jnp.float32),
            pltpu.VMEM((1, width), jnp.float32),
            pltpu.VMEM((HEADS, 1, width), jnp.float32),
            pltpu.VMEM((8, width), jnp.float32),
            dma((6,)),
            dma((2, 4)),
            dma((2, 4)),
            dma((2,)),
            dma((2,)),
            dma((1,)),
            dma((HEADS,)),
            dma((HEADS,)),
            dma((1,)),
            dma((11,)),
            dma((11,)),
            dma((HEADS,)),
            dma((HEADS,)),
            pltpu.SemaphoreType.REGULAR((4,)),
            pltpu.SemaphoreType.REGULAR((HEADS,)),
        ],
        compiler_params=pltpu.CompilerParams(
            collective_id=0, has_side_effects=True, vmem_limit_bytes=60 << 20
        ),
    )(
        queries.reshape(tok, width),
        keys.reshape(tok, width),
        values.reshape(tok, width),
        grad_out.reshape(tok, width),
        gain.reshape(1, share),
        doc_start,
        win_start,
    )
    grads = pl.pallas_call(
        deliver,
        out_shape=[jax.ShapeDtypeStruct(grad.shape, grad.dtype) for grad in grads],
        in_specs=[hbm] * 4,
        out_specs=[hbm] * 4,
        scratch_shapes=[pltpu.VMEM(grad.shape, grad.dtype) for grad in grads] + [dma((2, 4))],
        compiler_params=pltpu.CompilerParams(vmem_limit_bytes=60 << 20),
    )(*grads)
    shape = (1, tok, width)
    return (
        grads[0].reshape(shape),
        grads[1].reshape(shape),
        grads[2].reshape(shape),
        grads[3].reshape(share),
    )


def solution(mesh):
    rows = P("dp", "ctx", None)
    return jax.shard_map(
        on_device,
        mesh=mesh,
        in_specs=(rows, rows, rows, rows, P("dp"), P(), P()),
        out_specs=(rows, rows, rows, P("dp")),
        check_vma=False,
    )
```

```python
import functools
import math

import jax
import jax.numpy as jnp
from jax import lax
from jax.experimental import pallas as pl
from jax.experimental.pallas import tpu as pltpu
from jax.sharding import PartitionSpec as P

HEADS = 8
BLK = 128
WBLK = 8
HALO = (WBLK - 1) * BLK
STEP = 2 * BLK
PIECE = HALO // 4
MESH = pl.DeviceIdType.MESH
NEG = -1e30


def send(source, target, send_sem, recv_sem, device):
    return pltpu.make_async_remote_copy(
        src_ref=source,
        dst_ref=target,
        send_sem=send_sem,
        recv_sem=recv_sem,
        device_id=device,
        device_id_type=MESH,
    )


def body(
    n_ctx,
    q_hbm, k_hbm, v_hbm, g_hbm, share_ref, doc_hbm, win_hbm,
    dq_ref, dk_ref, dv_ref, gg_ref,
    q_ref, go_ref, k_ext, v_ext, k_t, scaled, doc_ref, win_ref, low_ref,
    s_scr, p_scr, dp_scr, ds_scr, dk_acc, dv_acc,
    dk_out, dv_out, dk_in, dv_in,
    gain_ref, gain_row, gain_in, gain_full, part_rows, part_in, head_row, head_in, part_acc,
    load_sem, halo_send, halo_recv, back_send, back_recv,
    gain_send, gain_recv, relay_send, relay_recv, part_send, part_recv, head_send, head_recv, met, met_rows,
):
    tok = q_ref.shape[0]
    width = q_ref.shape[1]
    groups = tok // STEP
    window = STEP + HALO
    kblocks = window // BLK
    score_scale = 1.0 / math.sqrt(width)
    exp_scale = score_scale * math.log2(math.e)
    c = lax.axis_index("ctx")
    d = lax.axis_index("dp")
    row = d // HEADS
    mine = d % HEADS
    diagonal = row == mine

    root = HEADS * row + row
    along = n_ctx // 2
    y = c % along
    y_base = c - y
    far_x = (c + along) % n_ctx
    y_peers = [y_base + (y + hop + along) % along for hop in (2, -2, 1, -1)]
    at_end = (y == 0) | (y == along - 1)
    half = HEADS // 2

    def source_of(other):
        near = jnp.where(other < mine, other + 1, mine)
        late = jnp.where(other < half, mine, near)
        start = jnp.where(other > mine, other - 1, mine)
        early = jnp.where(other < half, start, jnp.where(other < half + 2, half - 1, 0))
        return jnp.where(mine >= half, late, early)

    source = source_of(row)
    asked = source < row
    feeds = [(source_of(jnp.int32(t)) == row) & (row != t) for t in range(HEADS)]

    barrier = pltpu.get_barrier_semaphore()

    def greet(device):
        pl.semaphore_signal(barrier, inc=1, device_id=device, device_id_type=MESH)

    @pl.when(c > 0)
    def _():
        greet({"ctx": c - 1})

    @pl.when(at_end)
    def _():
        greet({"ctx": y_base + along - 1 - y})

    @pl.when(c < along)
    def _():
        greet({"ctx": far_x})

    @pl.when(diagonal)
    def _():
        for other in range(1, HEADS):
            greet({"dp": HEADS * row + (row + other) % HEADS})

    @pl.when(row < source)
    def _():
        greet({"dp": HEADS * source + mine})

    for t in range(HEADS):

        @pl.when(feeds[t] & (row < t))
        def _():
            greet({"dp": HEADS * t + mine})

    first_row = pl.multiple_of(c * tok, tok)
    loads = [
        pltpu.make_async_copy(k_hbm, k_ext.at[pl.ds(HALO, tok)], load_sem.at[0]),
        pltpu.make_async_copy(v_hbm, v_ext.at[pl.ds(HALO, tok)], load_sem.at[1]),
        pltpu.make_async_copy(q_hbm, q_ref, load_sem.at[2]),
        pltpu.make_async_copy(g_hbm, go_ref, load_sem.at[3]),
        pltpu.make_async_copy(doc_hbm.at[:, pl.ds(first_row, tok)], doc_ref, load_sem.at[4]),
        pltpu.make_async_copy(win_hbm.at[:, pl.ds(first_row, tok)], win_ref, load_sem.at[5]),
    ]
    gain_ref[...] = jnp.zeros_like(gain_ref)
    for load in loads:
        load.start()

    @pl.when(c == 0)
    def _():
        k_ext[pl.ds(0, HALO)] = jnp.zeros((HALO, width), k_ext.dtype)
        v_ext[pl.ds(0, HALO)] = jnp.zeros((HALO, width), v_ext.dtype)

    dk_acc[...] = jnp.zeros_like(dk_acc)
    dv_acc[...] = jnp.zeros_like(dv_acc)
    part_acc[...] = jnp.zeros_like(part_acc)

    gain_ref[:, 0 : share_ref.shape[1]] = share_ref[...]
    gain_row[...] = pltpu.roll(gain_ref[...], 16 * mine, 1)

    terms = [c < n_ctx - 1, at_end, c >= along, jnp.logical_not(diagonal), asked]
    terms += [feeds[t] & (row > t) for t in range(HEADS)]
    pl.semaphore_wait(barrier, sum(jnp.where(term, 1, 0) for term in terms))

    def halo_copy(which, piece, source, target):
        return send(
            source.at[pl.ds(tok - HALO + piece * PIECE, PIECE)],
            target.at[pl.ds(piece * PIECE, PIECE)],
            halo_send.at[which, piece],
            halo_recv.at[which, piece],
            {"ctx": c + 1},
        )

    to_root = send(gain_row, gain_in.at[mine], gain_send.at[0], gain_recv.at[mine], {"dp": root})

    def feed(t):
        return send(
            gain_full, gain_full, relay_send.at[t], relay_recv.at[0], {"dp": HEADS * t + mine}
        )


    @pl.when(jnp.logical_not(diagonal))
    def _():
        to_root.start()

    @pl.when(asked)
    def _():
        pl.semaphore_signal(
            met_rows.at[row], inc=1, device_id={"dp": HEADS * source + mine}, device_id_type=MESH
        )

    @pl.when(c >= along)
    def _():
        pl.semaphore_signal(met.at[2], inc=1, device_id={"ctx": far_x}, device_id_type=MESH)

    @pl.when(c < n_ctx - 1)
    def _():
        for piece in (3, 2, 1, 0):
            halo_copy(0, piece, k_hbm, k_ext).start()

    first_core = (d % 2 == 0) | (c == 0)

    def send_values():
        for piece in (3, 2, 1, 0):
            halo_copy(1, piece, v_hbm, v_ext).start()

    @pl.when((c < n_ctx - 1) & first_core)
    def _():
        send_values()

    hands_on = sum(jnp.where(feed_t, 1, 0) for feed_t in feeds) > 0

    @pl.when(diagonal)
    def _():
        total = gain_row[...]
        for other in range(1, HEADS):
            piece = (row + other) % HEADS
            send(
                gain_row, gain_in.at[piece], gain_send.at[0], gain_recv.at[piece], {"dp": HEADS * row + piece}
            ).wait_recv()
            total = total + gain_in[piece]
        gain_full[...] = total

    @pl.when(jnp.logical_not(diagonal) & hands_on)
    def _():
        feed(0).wait_recv()

    for t in range(HEADS):

        @pl.when(feeds[t] & (row < t))
        def _():
            pl.semaphore_wait(met_rows.at[t], 1)

        @pl.when(feeds[t])
        def _():
            feed(t).start()

    loads[4].wait()
    loads[5].wait()
    low_ref[...] = jnp.maximum(doc_ref[...], win_ref[...]) - (c * tok - HALO)
    loads[0].wait()
    for block in range(WBLK - 1, WBLK - 1 + tok // BLK):
        k_t[:, pl.ds(block * BLK, BLK)] = k_ext[pl.ds(block * BLK, BLK)].T
    loads[1].wait()
    loads[2].wait()
    loads[3].wait()


    seq = row

    def halo_arrives(which, group, source, target):
        @pl.when(c > 0)
        def _():
            halo_copy(which, group, source, target).wait_recv()

    def dot_nt(left, right):
        return lax.dot_general(
            left, right, (((1,), (1,)), ((), ())), preferred_element_type=jnp.float32
        )

    def chunk(at):
        return pl.ds(at * BLK, BLK)

    def chunk(at):
        return pl.ds(at * BLK, BLK)

    @pl.when(c > 0)
    def _():
        for piece in range(4):
            halo_copy(0, piece, k_hbm, k_ext).wait_recv()

    @pl.when((c < n_ctx - 1) & jnp.logical_not(first_core))
    def _():
        send_values()

    pl.semaphore_signal(met.at[0], inc=1, device_id={"ctx": y_peers[2]}, device_id_type=MESH)
    pl.semaphore_signal(met.at[1], inc=1, device_id={"ctx": y_peers[3]}, device_id_type=MESH)
    for block in range(WBLK - 1):
        k_t[:, pl.ds(block * BLK, BLK)] = k_ext[pl.ds(block * BLK, BLK)].T

    def prob_grad_step(step, carry):
        group = groups - 1 - step
        base = pl.multiple_of(group * STEP, STEP)
        halo_arrives(1, group, v_hbm, v_ext)
        dp_scr[group] = dot_nt(v_ext[pl.ds(base, window)], go_ref[pl.ds(base, STEP)])
        return carry

    lax.fori_loop(0, groups, prob_grad_step, 0)

    pl.semaphore_wait(met.at[0], 1)
    pl.semaphore_wait(met.at[1], 1)

    @pl.when(c < along)
    def _():
        pl.semaphore_wait(met.at[2], 1)

    pl.semaphore_signal(met.at[3], inc=1, device_id={"ctx": far_x}, device_id_type=MESH)

    @pl.when(jnp.logical_not(diagonal | hands_on))
    def _():
        feed(0).wait_recv()

    gain_all = gain_full[...]
    scaled[...] = (q_ref[...].astype(jnp.float32) * gain_all).astype(scaled.dtype)

    def query_step(step, carry):
        group = groups - 1 - step
        base = pl.multiple_of(group * STEP, STEP)
        s_scr[...] = dot_nt(k_ext[pl.ds(base, window)], scaled[pl.ds(base, STEP)])
        lower = low_ref[pl.ds(seq, 1), pl.ds(base, STEP)] - base
        key_row = lax.broadcasted_iota(jnp.int32, (BLK, STEP), 0)
        query_row = lax.broadcasted_iota(jnp.int32, (BLK, STEP), 1)
        highest = jnp.full((8, STEP), NEG, jnp.float32)
        for kb in range(kblocks):
            seen = key_row >= lower - kb * BLK
            if kb >= WBLK - 1:
                seen = seen & (key_row <= query_row + (HALO - kb * BLK))
            scores = jnp.where(seen, s_scr[chunk(kb)], NEG)
            s_scr[chunk(kb)] = scores
            highest = jnp.maximum(highest, jnp.max(scores.reshape(BLK // 8, 8, STEP), axis=0))
        highest = jnp.max(highest, axis=0, keepdims=True) * exp_scale
        total = jnp.zeros((8, STEP), jnp.float32)
        for kb in range(kblocks):
            weights = jnp.exp2(s_scr[chunk(kb)] * exp_scale - highest)
            s_scr[chunk(kb)] = weights
            total = total + jnp.sum(weights.reshape(BLK // 8, 8, STEP), axis=0)
        inverse = 1.0 / jnp.sum(total, axis=0, keepdims=True)
        delta = jnp.zeros((8, STEP), jnp.float32)
        for kb in range(kblocks):
            probs = (s_scr[chunk(kb)] * inverse).astype(p_scr.dtype)
            p_scr[group, chunk(kb)] = probs
            products = dp_scr[group, chunk(kb)] * probs.astype(jnp.float32)
            delta = delta + jnp.sum(products.reshape(BLK // 8, 8, STEP), axis=0)
        delta = jnp.sum(delta, axis=0, keepdims=True)
        for kb in range(kblocks):
            probs = p_scr[group, chunk(kb)].astype(jnp.float32)
            ds_scr[group, chunk(kb)] = (probs * (dp_scr[group, chunk(kb)] - delta)).astype(
                ds_scr.dtype
            )
        mixed_t = jnp.dot(
            k_t[:, pl.ds(base, window)], ds_scr[group], preferred_element_type=jnp.float32
        )
        mixed = mixed_t.T * score_scale
        dq_ref[pl.ds(base, STEP)] = (mixed * gain_all).astype(dq_ref.dtype)
        products = mixed * q_ref[pl.ds(base, STEP)].astype(jnp.float32)
        part_acc[...] += jnp.sum(products.reshape(STEP // 8, 8, width), axis=0)
        return carry

    lax.fori_loop(0, groups, query_step, 0, unroll=True)

    back_dv = send(dv_out, dv_in, back_send.at[0], back_recv.at[0], {"ctx": c - 1})
    back_dk = send(dk_out, dk_in, back_send.at[1], back_recv.at[1], {"ctx": c - 1})

    def key_grads():
        def step(group, carry):
            base = pl.multiple_of(group * STEP, STEP)
            dk_acc[pl.ds(base, window)] += jnp.dot(
                ds_scr[group], scaled[pl.ds(base, STEP)], preferred_element_type=jnp.float32
            )
            return carry

        lax.fori_loop(0, groups, step, 0)
        dk_out[...] = (dk_acc[pl.ds(0, HALO)] * score_scale).astype(dk_out.dtype)

        @pl.when(c > 0)
        def _():
            back_dk.start()

    def value_grads():
        def step(group, carry):
            base = pl.multiple_of(group * STEP, STEP)
            dv_acc[pl.ds(base, window)] += jnp.dot(
                p_scr[group], go_ref[pl.ds(base, STEP)], preferred_element_type=jnp.float32
            )
            return carry

        lax.fori_loop(0, groups, step, 0)
        dv_out[...] = dv_acc[pl.ds(0, HALO)].astype(dv_out.dtype)

        @pl.when(c > 0)
        def _():
            back_dv.start()

    part_rows[0] = jnp.sum(part_acc[...], axis=0, keepdims=True)

    def part_copy(source, slot, target):
        return send(source, part_in.at[slot], part_send.at[slot], part_recv.at[slot], {"ctx": target})

    x_peers = [(peer + along) % n_ctx for peer in y_peers]
    targets = x_peers + y_peers + [far_x]
    spread = [part_copy(part_rows.at[0], at, target) for at, target in enumerate(targets)]
    on_up = part_copy(part_rows.at[1], 9, y_peers[0])
    on_down = part_copy(part_rows.at[2], 10, y_peers[1])
    pl.semaphore_wait(met.at[3], 1)
    for copy in spread:
        copy.start()
    value_grads()
    key_grads()
    spread[2].wait_recv()
    spread[6].wait_recv()
    part_rows[1] = part_in[2] + part_in[6]
    on_up.start()
    for at in (1, 3, 5, 7):
        spread[at].wait_recv()
    part_rows[2] = part_in[1] + part_in[3] + part_in[5] + part_in[7]
    on_down.start()
    own_dk = dk_acc[pl.ds(HALO, tok)] * score_scale
    dk_acc[pl.ds(HALO, tok)] = own_dk
    dk_ref[...] = own_dk.astype(dk_ref.dtype)
    dv_ref[...] = dv_acc[pl.ds(HALO, tok)].astype(dv_ref.dtype)
    for at in (0, 4, 8):
        spread[at].wait_recv()
    across = part_rows[0] + part_in[8] + part_rows[1] + part_rows[2] + part_in[0] + part_in[4]
    on_up.wait_recv()
    on_down.wait_recv()
    head_row[...] = across + part_in[9] + part_in[10]

    def head_copy(target, slot):
        return send(head_row, head_in.at[row], head_send.at[slot], head_recv.at[row], {"dp": target})

    for other in range(HEADS):
        owner = HEADS * mine + other

        @pl.when(owner != d)
        def _():
            head_copy(owner, other).start()

        @pl.when(owner == d)
        def _():
            head_in[row] = head_row[...]

    @pl.when(c < n_ctx - 1)
    def _():
        back_dv.wait_recv()

    @pl.when(c < n_ctx - 1)
    def _():
        dv_ref[pl.ds(tok - HALO, HALO)] = (
            dv_acc[pl.ds(tok, HALO)] + dv_in[...].astype(jnp.float32)
        ).astype(dv_ref.dtype)
        back_dk.wait_recv()
        dk_ref[pl.ds(tok - HALO, HALO)] = (
            dk_acc[pl.ds(tok, HALO)] + dk_in[...].astype(jnp.float32)
        ).astype(dk_ref.dtype)

    for other in range(HEADS):
        user = row + HEADS * other

        @pl.when(user != d)
        def _():
            send(
                head_row, head_in.at[other], head_send.at[0], head_recv.at[other], {"dp": user}
            ).wait_recv()

    whole = head_in[0]
    for other in range(1, HEADS):
        whole = whole + head_in[other]
    whole = pltpu.roll(jnp.broadcast_to(whole, (8, width)), (width - 16 * mine) % width, 1)
    gg_ref[...] = whole[0:1, 0 : gg_ref.shape[1]]

    for other in range(HEADS):
        owner = HEADS * mine + other

        @pl.when(owner != d)
        def _():
            head_copy(owner, other).wait_send()

    for copy in [*spread, on_up, on_down]:
        copy.wait_send()

    @pl.when(jnp.logical_not(diagonal))
    def _():
        to_root.wait_send()

    for t in range(HEADS):

        @pl.when(feeds[t])
        def _():
            feed(t).wait_send()

    @pl.when(c < n_ctx - 1)
    def _():
        for piece in range(4):
            halo_copy(0, piece, k_hbm, k_ext).wait_send()
            halo_copy(1, piece, v_hbm, v_ext).wait_send()

    @pl.when(c > 0)
    def _():
        back_dv.wait_send()
        back_dk.wait_send()


def deliver(*refs):
    sources, targets, held, sems = refs[:4], refs[4:8], refs[8:12], refs[12]
    loads = [
        pltpu.make_async_copy(source, hold, sems.at[0, at])
        for at, (source, hold) in enumerate(zip(sources, held))
    ]
    stores = [
        pltpu.make_async_copy(hold, target, sems.at[1, at])
        for at, (target, hold) in enumerate(zip(targets, held))
    ]
    for load in loads:
        load.start()
    for load, store in zip(loads, stores):
        load.wait()
        store.start()
    for store in stores:
        store.wait()


def on_device(queries, keys, values, grad_out, gain, doc_start, win_start):
    _, tok, width = queries.shape
    n_ctx = lax.axis_size("ctx")
    seqs = doc_start.shape[0]
    share = gain.shape[0]
    window = STEP + HALO
    groups = tok // STEP
    wide = (HALO + tok, width)
    hbm = pl.BlockSpec(memory_space=pl.ANY)
    vmem = pl.BlockSpec(memory_space=pltpu.VMEM)
    dma = pltpu.SemaphoreType.DMA


    grads = pl.pallas_call(
        functools.partial(body, n_ctx),
        out_shape=[jax.ShapeDtypeStruct((tok, width), jnp.bfloat16)] * 3
        + [jax.ShapeDtypeStruct((1, share), jnp.float32)],
        in_specs=[hbm] * 4 + [vmem] + [hbm] * 2,
        out_specs=[vmem] * 4,
        scratch_shapes=[
            pltpu.VMEM((tok, width), jnp.bfloat16),
            pltpu.VMEM((tok, width), jnp.bfloat16),
            pltpu.VMEM(wide, jnp.bfloat16),
            pltpu.VMEM(wide, jnp.bfloat16),
            pltpu.VMEM((width, HALO + tok), jnp.bfloat16),
            pltpu.VMEM((tok, width), jnp.bfloat16),
            pltpu.VMEM((seqs, tok), jnp.int32),
            pltpu.VMEM((seqs, tok), jnp.int32),
            pltpu.VMEM((seqs, tok), jnp.int32),
            pltpu.VMEM((window, STEP), jnp.float32),
            pltpu.VMEM((groups, window, STEP), jnp.bfloat16),
            pltpu.VMEM((groups, window, STEP), jnp.float32),
            pltpu.VMEM((groups, window, STEP), jnp.bfloat16),
            pltpu.VMEM(wide, jnp.float32),
            pltpu.VMEM(wide, jnp.float32),
            pltpu.VMEM((HALO, width), jnp.bfloat16),
            pltpu.VMEM((HALO, width), jnp.bfloat16),
            pltpu.VMEM((HALO, width), jnp.bfloat16),
            pltpu.VMEM((HALO, width), jnp.bfloat16),
            pltpu.VMEM((1, width), jnp.float32),
            pltpu.VMEM((1, width), jnp.float32),
            pltpu.VMEM((HEADS, 1, width), jnp.float32),
            pltpu.VMEM((1, width), jnp.float32),
            pltpu.VMEM((3, 1, width), jnp.float32),
            pltpu.VMEM((11, 1, width), jnp.float32),
            pltpu.VMEM((1, width), jnp.float32),
            pltpu.VMEM((HEADS, 1, width), jnp.float32),
            pltpu.VMEM((8, width), jnp.float32),
            dma((6,)),
            dma((2, 4)),
            dma((2, 4)),
            dma((2,)),
            dma((2,)),
            dma((1,)),
            dma((HEADS,)),
            dma((HEADS,)),
            dma((1,)),
            dma((11,)),
            dma((11,)),
            dma((HEADS,)),
            dma((HEADS,)),
            pltpu.SemaphoreType.REGULAR((4,)),
            pltpu.SemaphoreType.REGULAR((HEADS,)),
        ],
        compiler_params=pltpu.CompilerParams(
            collective_id=0, has_side_effects=True, vmem_limit_bytes=60 << 20
        ),
    )(
        queries.reshape(tok, width),
        keys.reshape(tok, width),
        values.reshape(tok, width),
        grad_out.reshape(tok, width),
        gain.reshape(1, share),
        doc_start,
        win_start,
    )
    grads = pl.pallas_call(
        deliver,
        out_shape=[jax.ShapeDtypeStruct(grad.shape, grad.dtype) for grad in grads],
        in_specs=[hbm] * 4,
        out_specs=[hbm] * 4,
        scratch_shapes=[pltpu.VMEM(grad.shape, grad.dtype) for grad in grads] + [dma((2, 4))],
        compiler_params=pltpu.CompilerParams(vmem_limit_bytes=60 << 20),
    )(*grads)
    shape = (1, tok, width)
    return (
        grads[0].reshape(shape),
        grads[1].reshape(shape),
        grads[2].reshape(shape),
        grads[3].reshape(share),
    )


def solution(mesh):
    rows = P("dp", "ctx", None)
    return jax.shard_map(
        on_device,
        mesh=mesh,
        in_specs=(rows, rows, rows, rows, P("dp"), P(), P()),
        out_specs=(rows, rows, rows, P("dp")),
        check_vma=False,
    )
```

```python
import functools
import math

import jax
import jax.numpy as jnp
from jax import lax
from jax.experimental import pallas as pl
from jax.experimental.pallas import tpu as pltpu
from jax.sharding import PartitionSpec as P

HEADS = 8
BLK = 128
WBLK = 8
HALO = (WBLK - 1) * BLK
STEP = 2 * BLK
PIECE = HALO // 4
MESH = pl.DeviceIdType.MESH
NEG = -1e30


def send(source, target, send_sem, recv_sem, device):
    return pltpu.make_async_remote_copy(
        src_ref=source,
        dst_ref=target,
        send_sem=send_sem,
        recv_sem=recv_sem,
        device_id=device,
        device_id_type=MESH,
    )


def body(
    n_ctx,
    q_hbm, k_hbm, v_hbm, g_hbm, share_ref, doc_hbm, win_hbm,
    dq_ref, dk_ref, dv_ref, gg_ref,
    q_ref, go_ref, k_ext, v_ext, k_t, scaled, doc_ref, win_ref, low_ref,
    s_scr, p_scr, dp_scr, ds_scr, dk_acc, dv_acc,
    dk_out, dv_out, dk_in, dv_in,
    gain_ref, gain_row, gain_in, gain_full, part_rows, part_in, head_row, head_in, part_acc,
    load_sem, halo_send, halo_recv, back_send, back_recv,
    gain_send, gain_recv, relay_send, relay_recv, part_send, part_recv, head_send, head_recv, met, met_rows, here,
):
    tok = q_ref.shape[0]
    width = q_ref.shape[1]
    groups = tok // STEP
    window = STEP + HALO
    kblocks = window // BLK
    score_scale = 1.0 / math.sqrt(width)
    exp_scale = score_scale * math.log2(math.e)
    c = lax.axis_index("ctx")
    d = lax.axis_index("dp")
    row = d // HEADS
    mine = d % HEADS
    diagonal = row == mine

    root = HEADS * row + row
    along = n_ctx // 2
    y = c % along
    y_base = c - y
    far_x = (c + along) % n_ctx
    y_peers = [y_base + (y + hop + along) % along for hop in (2, -2, 1, -1)]
    at_end = (y == 0) | (y == along - 1)
    half = HEADS // 2

    def source_of(other):
        near = jnp.where(other < mine, other + 1, mine)
        late = jnp.where(other < half, mine, near)
        start = jnp.where(other > mine, other - 1, mine)
        early = jnp.where(other < half, start, jnp.where(other < half + 2, half - 1, 0))
        return jnp.where(mine >= half, late, early)

    source = source_of(row)
    asked = source < row
    feeds = [(source_of(jnp.int32(t)) == row) & (row != t) for t in range(HEADS)]

    barrier = pltpu.get_barrier_semaphore()

    def greet(device):
        pl.semaphore_signal(barrier, inc=1, device_id=device, device_id_type=MESH)

    @pl.when(c > 0)
    def _():
        greet({"ctx": c - 1})

    @pl.when(at_end)
    def _():
        greet({"ctx": y_base + along - 1 - y})

    @pl.when(c < along)
    def _():
        greet({"ctx": far_x})

    @pl.when(diagonal)
    def _():
        for other in range(1, HEADS):
            greet({"dp": HEADS * row + (row + other) % HEADS})

    @pl.when(row < source)
    def _():
        greet({"dp": HEADS * source + mine})

    for t in range(HEADS):

        @pl.when(feeds[t] & (row < t))
        def _():
            greet({"dp": HEADS * t + mine})

    first_row = pl.multiple_of(c * tok, tok)
    loads = [
        pltpu.make_async_copy(k_hbm, k_ext.at[pl.ds(HALO, tok)], load_sem.at[0]),
        pltpu.make_async_copy(v_hbm, v_ext.at[pl.ds(HALO, tok)], load_sem.at[1]),
        pltpu.make_async_copy(q_hbm, q_ref, load_sem.at[2]),
        pltpu.make_async_copy(g_hbm, go_ref, load_sem.at[3]),
        pltpu.make_async_copy(doc_hbm.at[:, pl.ds(first_row, tok)], doc_ref, load_sem.at[4]),
        pltpu.make_async_copy(win_hbm.at[:, pl.ds(first_row, tok)], win_ref, load_sem.at[5]),
    ]
    gain_ref[...] = jnp.zeros_like(gain_ref)
    for load in loads:
        load.start()

    @pl.when(c == 0)
    def _():
        k_ext[pl.ds(0, HALO)] = jnp.zeros((HALO, width), k_ext.dtype)
        v_ext[pl.ds(0, HALO)] = jnp.zeros((HALO, width), v_ext.dtype)

    dk_acc[...] = jnp.zeros_like(dk_acc)
    dv_acc[...] = jnp.zeros_like(dv_acc)
    part_acc[...] = jnp.zeros_like(part_acc)

    gain_ref[:, 0 : share_ref.shape[1]] = share_ref[...]
    gain_row[...] = pltpu.roll(gain_ref[...], 16 * mine, 1)

    terms = [c < n_ctx - 1, at_end, c >= along, jnp.logical_not(diagonal), asked]
    terms += [feeds[t] & (row > t) for t in range(HEADS)]
    pl.semaphore_wait(barrier, sum(jnp.where(term, 1, 0) for term in terms))

    def halo_copy(which, piece, source, target):
        return send(
            source.at[pl.ds(tok - HALO + piece * PIECE, PIECE)],
            target.at[pl.ds(piece * PIECE, PIECE)],
            halo_send.at[which, piece],
            halo_recv.at[which, piece],
            {"ctx": c + 1},
        )

    to_root = send(gain_row, gain_in.at[mine], gain_send.at[0], gain_recv.at[mine], {"dp": root})

    def feed(t):
        return send(
            gain_full, gain_full, relay_send.at[t], relay_recv.at[0], {"dp": HEADS * t + mine}
        )


    @pl.when(jnp.logical_not(diagonal))
    def _():
        to_root.start()

    @pl.when(asked)
    def _():
        pl.semaphore_signal(
            met_rows.at[row], inc=1, device_id={"dp": HEADS * source + mine}, device_id_type=MESH
        )

    @pl.when(c >= along)
    def _():
        pl.semaphore_signal(met.at[2], inc=1, device_id={"ctx": far_x}, device_id_type=MESH)

    @pl.when(c < n_ctx - 1)
    def _():
        for piece in (3, 2, 1, 0):
            halo_copy(0, piece, k_hbm, k_ext).start()

    first_core = (d % 2 == 0) | (c == 0)

    def send_values():
        for piece in (3, 2, 1, 0):
            halo_copy(1, piece, v_hbm, v_ext).start()

    @pl.when((c < n_ctx - 1) & first_core)
    def _():
        send_values()

    hands_on = sum(jnp.where(feed_t, 1, 0) for feed_t in feeds) > 0

    @pl.when(diagonal)
    def _():
        total = gain_row[...]
        for other in range(1, HEADS):
            piece = (row + other) % HEADS
            send(
                gain_row, gain_in.at[piece], gain_send.at[0], gain_recv.at[piece], {"dp": HEADS * row + piece}
            ).wait_recv()
            total = total + gain_in[piece]
        gain_full[...] = total

    @pl.when(jnp.logical_not(diagonal) & hands_on)
    def _():
        feed(0).wait_recv()

    aside = (mine == 0) & (c == 0)
    first_of_all = aside & (row == 0)
    hands_over = (mine == 0) & (c == 1) & (row == 1)
    sends = [feeds[t] & jnp.logical_not(first_of_all) if t == 1 else feeds[t] for t in range(HEADS)]
    over = send(gain_full, gain_full, relay_send.at[0], relay_recv.at[0], {"ctx": c - 1})

    def tell(t):
        pl.semaphore_signal(
            here.at[0], inc=1, device_id={"dp": HEADS * t + mine}, device_id_type=MESH
        )

    for t in range(HEADS):

        @pl.when(feeds[t] & (row < t))
        def _():
            pl.semaphore_wait(met_rows.at[t], 1)

        @pl.when(sends[t])
        def _():
            feed(t).start()

    @pl.when(first_of_all)
    def _():
        tell(1)

    loads[4].wait()
    loads[5].wait()
    low_ref[...] = jnp.maximum(doc_ref[...], win_ref[...]) - (c * tok - HALO)
    loads[0].wait()
    for block in range(WBLK - 1, WBLK - 1 + tok // BLK):
        k_t[:, pl.ds(block * BLK, BLK)] = k_ext[pl.ds(block * BLK, BLK)].T
    loads[1].wait()
    loads[2].wait()
    loads[3].wait()


    seq = row

    def halo_arrives(which, group, source, target):
        @pl.when(c > 0)
        def _():
            halo_copy(which, group, source, target).wait_recv()

    def dot_nt(left, right):
        return lax.dot_general(
            left, right, (((1,), (1,)), ((), ())), preferred_element_type=jnp.float32
        )

    def chunk(at):
        return pl.ds(at * BLK, BLK)

    def chunk(at):
        return pl.ds(at * BLK, BLK)

    @pl.when(c > 0)
    def _():
        for piece in range(4):
            halo_copy(0, piece, k_hbm, k_ext).wait_recv()

    @pl.when((c < n_ctx - 1) & jnp.logical_not(first_core))
    def _():
        send_values()

    @pl.when(hands_over)
    def _():
        over.start()

    pl.semaphore_signal(met.at[0], inc=1, device_id={"ctx": y_peers[2]}, device_id_type=MESH)
    pl.semaphore_signal(met.at[1], inc=1, device_id={"ctx": y_peers[3]}, device_id_type=MESH)
    for block in range(WBLK - 1):
        k_t[:, pl.ds(block * BLK, BLK)] = k_ext[pl.ds(block * BLK, BLK)].T

    @pl.when(jnp.logical_not(diagonal | hands_on))
    def _():
        feed(0).wait_recv()

    gain_all = gain_full[...]
    scaled[...] = (q_ref[...].astype(jnp.float32) * gain_all).astype(scaled.dtype)

    def query_step(step, carry):
        group = groups - 1 - step
        base = pl.multiple_of(group * STEP, STEP)
        s_scr[...] = dot_nt(k_ext[pl.ds(base, window)], scaled[pl.ds(base, STEP)])
        lower = low_ref[pl.ds(seq, 1), pl.ds(base, STEP)] - base
        key_row = lax.broadcasted_iota(jnp.int32, (BLK, STEP), 0)
        query_row = lax.broadcasted_iota(jnp.int32, (BLK, STEP), 1)
        highest = jnp.full((8, STEP), NEG, jnp.float32)
        for kb in range(kblocks):
            seen = key_row >= lower - kb * BLK
            if kb >= WBLK - 1:
                seen = seen & (key_row <= query_row + (HALO - kb * BLK))
            scores = jnp.where(seen, s_scr[chunk(kb)], NEG)
            s_scr[chunk(kb)] = scores
            highest = jnp.maximum(highest, jnp.max(scores.reshape(BLK // 8, 8, STEP), axis=0))
        highest = jnp.max(highest, axis=0, keepdims=True) * exp_scale
        total = jnp.zeros((8, STEP), jnp.float32)
        for kb in range(kblocks):
            weights = jnp.exp2(s_scr[chunk(kb)] * exp_scale - highest)
            s_scr[chunk(kb)] = weights
            total = total + jnp.sum(weights.reshape(BLK // 8, 8, STEP), axis=0)
        inverse = 1.0 / jnp.sum(total, axis=0, keepdims=True)
        for kb in range(kblocks):
            p_scr[group, chunk(kb)] = (s_scr[chunk(kb)] * inverse).astype(p_scr.dtype)
        return carry

    lax.fori_loop(0, groups, query_step, 0, unroll=True)

    pl.semaphore_wait(met.at[0], 1)
    pl.semaphore_wait(met.at[1], 1)

    @pl.when(c < along)
    def _():
        pl.semaphore_wait(met.at[2], 1)

    pl.semaphore_signal(met.at[3], inc=1, device_id={"ctx": far_x}, device_id_type=MESH)

    @pl.when(aside & (row >= 1) & (row < half))
    def _():
        pl.semaphore_wait(here.at[0], 1)

    @pl.when(aside & (row >= 1) & (row < half - 1))
    def _():
        tell(row + 1)

    @pl.when(aside & (row == half - 1))
    def _():
        tell(half)
        tell(half + 1)

    def grad_step(step, carry):
        group = groups - 1 - step
        base = pl.multiple_of(group * STEP, STEP)
        halo_arrives(1, group, v_hbm, v_ext)
        dp_scr[group] = dot_nt(v_ext[pl.ds(base, window)], go_ref[pl.ds(base, STEP)])
        delta = jnp.zeros((8, STEP), jnp.float32)
        for kb in range(kblocks):
            products = dp_scr[group, chunk(kb)] * p_scr[group, chunk(kb)].astype(jnp.float32)
            delta = delta + jnp.sum(products.reshape(BLK // 8, 8, STEP), axis=0)
        delta = jnp.sum(delta, axis=0, keepdims=True)
        for kb in range(kblocks):
            probs = p_scr[group, chunk(kb)].astype(jnp.float32)
            ds_scr[group, chunk(kb)] = (probs * (dp_scr[group, chunk(kb)] - delta)).astype(
                ds_scr.dtype
            )
        mixed_t = jnp.dot(
            k_t[:, pl.ds(base, window)], ds_scr[group], preferred_element_type=jnp.float32
        )
        mixed = mixed_t.T * score_scale
        dq_ref[pl.ds(base, STEP)] = (mixed * gain_all).astype(dq_ref.dtype)
        products = mixed * q_ref[pl.ds(base, STEP)].astype(jnp.float32)
        part_acc[...] += jnp.sum(products.reshape(STEP // 8, 8, width), axis=0)
        return carry

    lax.fori_loop(0, groups, grad_step, 0, unroll=True)

    back_dv = send(dv_out, dv_in, back_send.at[0], back_recv.at[0], {"ctx": c - 1})
    back_dk = send(dk_out, dk_in, back_send.at[1], back_recv.at[1], {"ctx": c - 1})

    def key_grads():
        def step(group, carry):
            base = pl.multiple_of(group * STEP, STEP)
            dk_acc[pl.ds(base, window)] += jnp.dot(
                ds_scr[group], scaled[pl.ds(base, STEP)], preferred_element_type=jnp.float32
            )
            return carry

        lax.fori_loop(0, groups, step, 0)
        dk_out[...] = (dk_acc[pl.ds(0, HALO)] * score_scale).astype(dk_out.dtype)

        @pl.when(c > 0)
        def _():
            back_dk.start()

    def value_grads():
        def step(group, carry):
            base = pl.multiple_of(group * STEP, STEP)
            dv_acc[pl.ds(base, window)] += jnp.dot(
                p_scr[group], go_ref[pl.ds(base, STEP)], preferred_element_type=jnp.float32
            )
            return carry

        lax.fori_loop(0, groups, step, 0)
        dv_out[...] = dv_acc[pl.ds(0, HALO)].astype(dv_out.dtype)

        @pl.when(c > 0)
        def _():
            back_dv.start()

    part_rows[0] = jnp.sum(part_acc[...], axis=0, keepdims=True)

    def part_copy(source, slot, target):
        return send(source, part_in.at[slot], part_send.at[slot], part_recv.at[slot], {"ctx": target})

    x_peers = [(peer + along) % n_ctx for peer in y_peers]
    targets = x_peers + y_peers + [far_x]
    spread = [part_copy(part_rows.at[0], at, target) for at, target in enumerate(targets)]
    on_up = part_copy(part_rows.at[1], 9, y_peers[0])
    on_down = part_copy(part_rows.at[2], 10, y_peers[1])
    pl.semaphore_wait(met.at[3], 1)
    for copy in spread:
        copy.start()
    value_grads()
    key_grads()
    spread[2].wait_recv()
    spread[6].wait_recv()
    part_rows[1] = part_in[2] + part_in[6]
    on_up.start()
    for at in (1, 3, 5, 7):
        spread[at].wait_recv()
    part_rows[2] = part_in[1] + part_in[3] + part_in[5] + part_in[7]
    on_down.start()
    own_dk = dk_acc[pl.ds(HALO, tok)] * score_scale
    dk_acc[pl.ds(HALO, tok)] = own_dk
    dk_ref[...] = own_dk.astype(dk_ref.dtype)
    dv_ref[...] = dv_acc[pl.ds(HALO, tok)].astype(dv_ref.dtype)
    for at in (0, 4, 8):
        spread[at].wait_recv()
    across = part_rows[0] + part_in[8] + part_rows[1] + part_rows[2] + part_in[0] + part_in[4]
    on_up.wait_recv()
    on_down.wait_recv()
    head_row[...] = across + part_in[9] + part_in[10]

    @pl.when(aside & ((row == half) | (row == half + 1)))
    def _():
        pl.semaphore_wait(here.at[0], 1)

    def head_copy(target, slot):
        return send(head_row, head_in.at[row], head_send.at[slot], head_recv.at[row], {"dp": target})

    for other in range(HEADS):
        owner = HEADS * mine + other

        @pl.when(owner != d)
        def _():
            head_copy(owner, other).start()

        @pl.when(owner == d)
        def _():
            head_in[row] = head_row[...]

    @pl.when(c < n_ctx - 1)
    def _():
        back_dv.wait_recv()

    @pl.when(c < n_ctx - 1)
    def _():
        dv_ref[pl.ds(tok - HALO, HALO)] = (
            dv_acc[pl.ds(tok, HALO)] + dv_in[...].astype(jnp.float32)
        ).astype(dv_ref.dtype)
        back_dk.wait_recv()
        dk_ref[pl.ds(tok - HALO, HALO)] = (
            dk_acc[pl.ds(tok, HALO)] + dk_in[...].astype(jnp.float32)
        ).astype(dk_ref.dtype)

    for other in range(HEADS):
        user = row + HEADS * other

        @pl.when(user != d)
        def _():
            send(
                head_row, head_in.at[other], head_send.at[0], head_recv.at[other], {"dp": user}
            ).wait_recv()

    whole = head_in[0]
    for other in range(1, HEADS):
        whole = whole + head_in[other]
    whole = pltpu.roll(jnp.broadcast_to(whole, (8, width)), (width - 16 * mine) % width, 1)
    gg_ref[...] = whole[0:1, 0 : gg_ref.shape[1]]

    for other in range(HEADS):
        owner = HEADS * mine + other

        @pl.when(owner != d)
        def _():
            head_copy(owner, other).wait_send()

    for copy in [*spread, on_up, on_down]:
        copy.wait_send()

    @pl.when(jnp.logical_not(diagonal))
    def _():
        to_root.wait_send()

    for t in range(HEADS):

        @pl.when(sends[t])
        def _():
            feed(t).wait_send()

    @pl.when(hands_over)
    def _():
        over.wait_send()

    @pl.when(c < n_ctx - 1)
    def _():
        for piece in range(4):
            halo_copy(0, piece, k_hbm, k_ext).wait_send()
            halo_copy(1, piece, v_hbm, v_ext).wait_send()

    @pl.when(c > 0)
    def _():
        back_dv.wait_send()
        back_dk.wait_send()


def deliver(*refs):
    sources, targets, held, sems = refs[:4], refs[4:8], refs[8:12], refs[12]
    loads = [
        pltpu.make_async_copy(source, hold, sems.at[0, at])
        for at, (source, hold) in enumerate(zip(sources, held))
    ]
    stores = [
        pltpu.make_async_copy(hold, target, sems.at[1, at])
        for at, (target, hold) in enumerate(zip(targets, held))
    ]
    for load in loads:
        load.start()
    for load, store in zip(loads, stores):
        load.wait()
        store.start()
    for store in stores:
        store.wait()


def on_device(queries, keys, values, grad_out, gain, doc_start, win_start):
    _, tok, width = queries.shape
    n_ctx = lax.axis_size("ctx")
    seqs = doc_start.shape[0]
    share = gain.shape[0]
    window = STEP + HALO
    groups = tok // STEP
    wide = (HALO + tok, width)
    hbm = pl.BlockSpec(memory_space=pl.ANY)
    vmem = pl.BlockSpec(memory_space=pltpu.VMEM)
    dma = pltpu.SemaphoreType.DMA


    grads = pl.pallas_call(
        functools.partial(body, n_ctx),
        out_shape=[jax.ShapeDtypeStruct((tok, width), jnp.bfloat16)] * 3
        + [jax.ShapeDtypeStruct((1, share), jnp.float32)],
        in_specs=[hbm] * 4 + [vmem] + [hbm] * 2,
        out_specs=[vmem] * 4,
        scratch_shapes=[
            pltpu.VMEM((tok, width), jnp.bfloat16),
            pltpu.VMEM((tok, width), jnp.bfloat16),
            pltpu.VMEM(wide, jnp.bfloat16),
            pltpu.VMEM(wide, jnp.bfloat16),
            pltpu.VMEM((width, HALO + tok), jnp.bfloat16),
            pltpu.VMEM((tok, width), jnp.bfloat16),
            pltpu.VMEM((seqs, tok), jnp.int32),
            pltpu.VMEM((seqs, tok), jnp.int32),
            pltpu.VMEM((seqs, tok), jnp.int32),
            pltpu.VMEM((window, STEP), jnp.float32),
            pltpu.VMEM((groups, window, STEP), jnp.bfloat16),
            pltpu.VMEM((groups, window, STEP), jnp.float32),
            pltpu.VMEM((groups, window, STEP), jnp.bfloat16),
            pltpu.VMEM(wide, jnp.float32),
            pltpu.VMEM(wide, jnp.float32),
            pltpu.VMEM((HALO, width), jnp.bfloat16),
            pltpu.VMEM((HALO, width), jnp.bfloat16),
            pltpu.VMEM((HALO, width), jnp.bfloat16),
            pltpu.VMEM((HALO, width), jnp.bfloat16),
            pltpu.VMEM((1, width), jnp.float32),
            pltpu.VMEM((1, width), jnp.float32),
            pltpu.VMEM((HEADS, 1, width), jnp.float32),
            pltpu.VMEM((1, width), jnp.float32),
            pltpu.VMEM((3, 1, width), jnp.float32),
            pltpu.VMEM((11, 1, width), jnp.float32),
            pltpu.VMEM((1, width), jnp.float32),
            pltpu.VMEM((HEADS, 1, width), jnp.float32),
            pltpu.VMEM((8, width), jnp.float32),
            dma((6,)),
            dma((2, 4)),
            dma((2, 4)),
            dma((2,)),
            dma((2,)),
            dma((1,)),
            dma((HEADS,)),
            dma((HEADS,)),
            dma((1,)),
            dma((11,)),
            dma((11,)),
            dma((HEADS,)),
            dma((HEADS,)),
            pltpu.SemaphoreType.REGULAR((4,)),
            pltpu.SemaphoreType.REGULAR((HEADS,)),
            pltpu.SemaphoreType.REGULAR((1,)),
        ],
        compiler_params=pltpu.CompilerParams(
            collective_id=0, has_side_effects=True, vmem_limit_bytes=60 << 20
        ),
    )(
        queries.reshape(tok, width),
        keys.reshape(tok, width),
        values.reshape(tok, width),
        grad_out.reshape(tok, width),
        gain.reshape(1, share),
        doc_start,
        win_start,
    )
    grads = pl.pallas_call(
        deliver,
        out_shape=[jax.ShapeDtypeStruct(grad.shape, grad.dtype) for grad in grads],
        in_specs=[hbm] * 4,
        out_specs=[hbm] * 4,
        scratch_shapes=[pltpu.VMEM(grad.shape, grad.dtype) for grad in grads] + [dma((2, 4))],
        compiler_params=pltpu.CompilerParams(vmem_limit_bytes=60 << 20),
    )(*grads)
    shape = (1, tok, width)
    return (
        grads[0].reshape(shape),
        grads[1].reshape(shape),
        grads[2].reshape(shape),
        grads[3].reshape(share),
    )


def solution(mesh):
    rows = P("dp", "ctx", None)
    return jax.shard_map(
        on_device,
        mesh=mesh,
        in_specs=(rows, rows, rows, rows, P("dp"), P(), P()),
        out_specs=(rows, rows, rows, P("dp")),
        check_vma=False,
    )
```

```python
import functools
import math

import jax
import jax.numpy as jnp
from jax import lax
from jax.experimental import pallas as pl
from jax.experimental.pallas import tpu as pltpu
from jax.sharding import PartitionSpec as P

HEADS = 8
BLK = 128
WBLK = 8
HALO = (WBLK - 1) * BLK
STEP = 2 * BLK
PIECE = HALO // 4
MESH = pl.DeviceIdType.MESH
NEG = -1e30


def send(source, target, send_sem, recv_sem, device):
    return pltpu.make_async_remote_copy(
        src_ref=source,
        dst_ref=target,
        send_sem=send_sem,
        recv_sem=recv_sem,
        device_id=device,
        device_id_type=MESH,
    )


def body(
    n_ctx,
    q_hbm, k_hbm, v_hbm, g_hbm, share_ref, doc_hbm, win_hbm,
    dq_ref, dk_ref, dv_ref, gg_ref,
    q_ref, go_ref, k_ext, v_ext, k_t, scaled, doc_ref, win_ref, low_ref,
    s_scr, p_scr, dp_scr, ds_scr, dk_acc, dv_acc,
    dk_out, dv_out, dk_in, dv_in,
    gain_ref, gain_row, gain_in, gain_full, part_rows, part_in, head_row, head_in, part_acc,
    load_sem, halo_send, halo_recv, back_send, back_recv,
    gain_send, gain_recv, relay_send, relay_recv, part_send, part_recv, head_send, head_recv, met, met_rows, here,
):
    tok = q_ref.shape[0]
    width = q_ref.shape[1]
    groups = tok // STEP
    window = STEP + HALO
    kblocks = window // BLK
    score_scale = 1.0 / math.sqrt(width)
    exp_scale = score_scale * math.log2(math.e)
    c = lax.axis_index("ctx")
    d = lax.axis_index("dp")
    row = d // HEADS
    mine = d % HEADS
    diagonal = row == mine

    root = HEADS * row + row
    along = n_ctx // 2
    y = c % along
    y_base = c - y
    far_x = (c + along) % n_ctx
    y_peers = [y_base + (y + hop + along) % along for hop in (2, -2, 1, -1)]
    at_end = (y == 0) | (y == along - 1)
    half = HEADS // 2

    def source_of(other):
        near = jnp.where(other < mine, other + 1, mine)
        late = jnp.where(other < half, mine, near)
        start = jnp.where(other > mine, other - 1, mine)
        early = jnp.where(other < half, start, jnp.where(other < half + 2, half - 1, 0))
        return jnp.where(mine >= half, late, early)

    source = source_of(row)
    asked = source < row
    feeds = [(source_of(jnp.int32(t)) == row) & (row != t) for t in range(HEADS)]

    barrier = pltpu.get_barrier_semaphore()

    def greet(device):
        pl.semaphore_signal(barrier, inc=1, device_id=device, device_id_type=MESH)

    @pl.when(c > 0)
    def _():
        greet({"ctx": c - 1})

    @pl.when(at_end)
    def _():
        greet({"ctx": y_base + along - 1 - y})

    @pl.when(c < along)
    def _():
        greet({"ctx": far_x})

    @pl.when(diagonal)
    def _():
        for other in range(1, HEADS):
            greet({"dp": HEADS * row + (row + other) % HEADS})

    @pl.when(row < source)
    def _():
        greet({"dp": HEADS * source + mine})

    for t in range(HEADS):

        @pl.when(feeds[t] & (row < t))
        def _():
            greet({"dp": HEADS * t + mine})

    first_row = pl.multiple_of(c * tok, tok)
    loads = [
        pltpu.make_async_copy(k_hbm, k_ext.at[pl.ds(HALO, tok)], load_sem.at[0]),
        pltpu.make_async_copy(v_hbm, v_ext.at[pl.ds(HALO, tok)], load_sem.at[1]),
        pltpu.make_async_copy(q_hbm, q_ref, load_sem.at[2]),
        pltpu.make_async_copy(g_hbm, go_ref, load_sem.at[3]),
        pltpu.make_async_copy(doc_hbm.at[:, pl.ds(first_row, tok)], doc_ref, load_sem.at[4]),
        pltpu.make_async_copy(win_hbm.at[:, pl.ds(first_row, tok)], win_ref, load_sem.at[5]),
    ]
    gain_ref[...] = jnp.zeros_like(gain_ref)
    for load in loads:
        load.start()

    @pl.when(c == 0)
    def _():
        k_ext[pl.ds(0, HALO)] = jnp.zeros((HALO, width), k_ext.dtype)
        v_ext[pl.ds(0, HALO)] = jnp.zeros((HALO, width), v_ext.dtype)

    dk_acc[...] = jnp.zeros_like(dk_acc)
    dv_acc[...] = jnp.zeros_like(dv_acc)
    part_acc[...] = jnp.zeros_like(part_acc)

    gain_ref[:, 0 : share_ref.shape[1]] = share_ref[...]
    gain_row[...] = pltpu.roll(gain_ref[...], 16 * mine, 1)

    terms = [c < n_ctx - 1, at_end, c >= along, jnp.logical_not(diagonal), asked]
    terms += [feeds[t] & (row > t) for t in range(HEADS)]
    pl.semaphore_wait(barrier, sum(jnp.where(term, 1, 0) for term in terms))

    def halo_copy(which, piece, source, target):
        return send(
            source.at[pl.ds(tok - HALO + piece * PIECE, PIECE)],
            target.at[pl.ds(piece * PIECE, PIECE)],
            halo_send.at[which, piece],
            halo_recv.at[which, piece],
            {"ctx": c + 1},
        )

    to_root = send(gain_row, gain_in.at[mine], gain_send.at[0], gain_recv.at[mine], {"dp": root})

    def feed(t):
        return send(
            gain_full, gain_full, relay_send.at[t], relay_recv.at[0], {"dp": HEADS * t + mine}
        )


    @pl.when(jnp.logical_not(diagonal))
    def _():
        to_root.start()

    @pl.when(asked)
    def _():
        pl.semaphore_signal(
            met_rows.at[row], inc=1, device_id={"dp": HEADS * source + mine}, device_id_type=MESH
        )

    @pl.when(c >= along)
    def _():
        pl.semaphore_signal(met.at[2], inc=1, device_id={"ctx": far_x}, device_id_type=MESH)

    @pl.when(c < n_ctx - 1)
    def _():
        for piece in (3, 2, 1, 0):
            halo_copy(0, piece, k_hbm, k_ext).start()

    first_core = (d % 2 == 0) | (c == 0)

    def send_values():
        for piece in (3, 2, 1, 0):
            halo_copy(1, piece, v_hbm, v_ext).start()

    @pl.when((c < n_ctx - 1) & first_core)
    def _():
        send_values()

    hands_on = sum(jnp.where(feed_t, 1, 0) for feed_t in feeds) > 0

    @pl.when(diagonal)
    def _():
        total = gain_row[...]
        for other in range(1, HEADS):
            piece = (row + other) % HEADS
            send(
                gain_row, gain_in.at[piece], gain_send.at[0], gain_recv.at[piece], {"dp": HEADS * row + piece}
            ).wait_recv()
            total = total + gain_in[piece]
        gain_full[...] = total

    @pl.when(jnp.logical_not(diagonal) & hands_on)
    def _():
        feed(0).wait_recv()

    aside = (mine == 0) & (c == 0)
    first_of_all = aside & (row == 0)
    hands_over = (mine == 0) & (c == 1) & (row == 1)
    sends = [feeds[t] & jnp.logical_not(first_of_all) if t == 1 else feeds[t] for t in range(HEADS)]
    over = send(gain_full, gain_full, relay_send.at[0], relay_recv.at[0], {"ctx": c - 1})

    def tell(t):
        pl.semaphore_signal(
            here.at[0], inc=1, device_id={"dp": HEADS * t + mine}, device_id_type=MESH
        )

    for t in range(HEADS):

        @pl.when(feeds[t] & (row < t))
        def _():
            pl.semaphore_wait(met_rows.at[t], 1)

        @pl.when(sends[t])
        def _():
            feed(t).start()

    @pl.when(first_of_all)
    def _():
        tell(1)

    loads[4].wait()
    loads[5].wait()
    low_ref[...] = jnp.maximum(doc_ref[...], win_ref[...]) - (c * tok - HALO)
    loads[0].wait()
    for block in range(WBLK - 1, WBLK - 1 + tok // BLK):
        k_t[:, pl.ds(block * BLK, BLK)] = k_ext[pl.ds(block * BLK, BLK)].T
    loads[1].wait()
    loads[2].wait()
    loads[3].wait()


    seq = row

    def halo_arrives(which, group, source, target):
        @pl.when(c > 0)
        def _():
            halo_copy(which, group, source, target).wait_recv()

    def dot_nt(left, right):
        return lax.dot_general(
            left, right, (((1,), (1,)), ((), ())), preferred_element_type=jnp.float32
        )

    def chunk(at):
        return pl.ds(at * BLK, BLK)

    def chunk(at):
        return pl.ds(at * BLK, BLK)

    @pl.when(c > 0)
    def _():
        for piece in range(4):
            halo_copy(0, piece, k_hbm, k_ext).wait_recv()

    @pl.when((c < n_ctx - 1) & jnp.logical_not(first_core))
    def _():
        send_values()

    @pl.when(hands_over)
    def _():
        over.start()

    pl.semaphore_signal(met.at[0], inc=1, device_id={"ctx": y_peers[2]}, device_id_type=MESH)
    pl.semaphore_signal(met.at[1], inc=1, device_id={"ctx": y_peers[3]}, device_id_type=MESH)
    for block in range(WBLK - 1):
        k_t[:, pl.ds(block * BLK, BLK)] = k_ext[pl.ds(block * BLK, BLK)].T

    @pl.when(jnp.logical_not(diagonal | hands_on))
    def _():
        feed(0).wait_recv()

    gain_all = gain_full[...]
    scaled[...] = (q_ref[...].astype(jnp.float32) * gain_all).astype(scaled.dtype)

    def query_step(step, carry):
        group = groups - 1 - step
        base = pl.multiple_of(group * STEP, STEP)
        s_scr[...] = dot_nt(k_ext[pl.ds(base, window)], scaled[pl.ds(base, STEP)])
        lower = low_ref[pl.ds(seq, 1), pl.ds(base, STEP)] - base
        key_row = lax.broadcasted_iota(jnp.int32, (BLK, STEP), 0)
        query_row = lax.broadcasted_iota(jnp.int32, (BLK, STEP), 1)
        highest = jnp.full((8, STEP), NEG, jnp.float32)
        for kb in range(kblocks):
            seen = key_row >= lower - kb * BLK
            if kb >= WBLK - 1:
                seen = seen & (key_row <= query_row + (HALO - kb * BLK))
            scores = jnp.where(seen, s_scr[chunk(kb)], NEG)
            s_scr[chunk(kb)] = scores
            highest = jnp.maximum(highest, jnp.max(scores.reshape(BLK // 8, 8, STEP), axis=0))
        highest = jnp.max(highest, axis=0, keepdims=True) * exp_scale
        total = jnp.zeros((8, STEP), jnp.float32)
        for kb in range(kblocks):
            weights = jnp.exp2(s_scr[chunk(kb)] * exp_scale - highest)
            s_scr[chunk(kb)] = weights
            total = total + jnp.sum(weights.reshape(BLK // 8, 8, STEP), axis=0)
        inverse = 1.0 / jnp.sum(total, axis=0, keepdims=True)
        for kb in range(kblocks):
            p_scr[group, chunk(kb)] = (s_scr[chunk(kb)] * inverse).astype(p_scr.dtype)
        return carry

    lax.fori_loop(0, groups, query_step, 0, unroll=True)

    back_dv = send(dv_out, dv_in, back_send.at[0], back_recv.at[0], {"ctx": c - 1})
    back_dk = send(dk_out, dk_in, back_send.at[1], back_recv.at[1], {"ctx": c - 1})

    def key_grads():
        def step(group, carry):
            base = pl.multiple_of(group * STEP, STEP)
            dk_acc[pl.ds(base, window)] += jnp.dot(
                ds_scr[group], scaled[pl.ds(base, STEP)], preferred_element_type=jnp.float32
            )
            return carry

        lax.fori_loop(0, groups, step, 0)
        dk_out[...] = (dk_acc[pl.ds(0, HALO)] * score_scale).astype(dk_out.dtype)

    def value_grads():
        def step(group, carry):
            base = pl.multiple_of(group * STEP, STEP)
            dv_acc[pl.ds(base, window)] += jnp.dot(
                p_scr[group], go_ref[pl.ds(base, STEP)], preferred_element_type=jnp.float32
            )
            return carry

        lax.fori_loop(0, groups, step, 0)
        dv_out[...] = dv_acc[pl.ds(0, HALO)].astype(dv_out.dtype)

        @pl.when(c > 0)
        def _():
            back_dv.start()

    value_grads()
    pl.semaphore_wait(met.at[0], 1)
    pl.semaphore_wait(met.at[1], 1)

    @pl.when(c < along)
    def _():
        pl.semaphore_wait(met.at[2], 1)

    pl.semaphore_signal(met.at[3], inc=1, device_id={"ctx": far_x}, device_id_type=MESH)

    @pl.when(aside & (row >= 1) & (row < half))
    def _():
        pl.semaphore_wait(here.at[0], 1)

    @pl.when(aside & (row >= 1) & (row < half - 1))
    def _():
        tell(row + 1)

    @pl.when(aside & (row == half - 1))
    def _():
        tell(half)
        tell(half + 1)

    def grad_step(step, carry):
        group = groups - 1 - step
        base = pl.multiple_of(group * STEP, STEP)
        halo_arrives(1, group, v_hbm, v_ext)
        dp_scr[group] = dot_nt(v_ext[pl.ds(base, window)], go_ref[pl.ds(base, STEP)])
        delta = jnp.zeros((8, STEP), jnp.float32)
        for kb in range(kblocks):
            products = dp_scr[group, chunk(kb)] * p_scr[group, chunk(kb)].astype(jnp.float32)
            delta = delta + jnp.sum(products.reshape(BLK // 8, 8, STEP), axis=0)
        delta = jnp.sum(delta, axis=0, keepdims=True)
        for kb in range(kblocks):
            probs = p_scr[group, chunk(kb)].astype(jnp.float32)
            ds_scr[group, chunk(kb)] = (probs * (dp_scr[group, chunk(kb)] - delta)).astype(
                ds_scr.dtype
            )
        mixed_t = jnp.dot(
            k_t[:, pl.ds(base, window)], ds_scr[group], preferred_element_type=jnp.float32
        )
        mixed = mixed_t.T * score_scale
        dq_ref[pl.ds(base, STEP)] = (mixed * gain_all).astype(dq_ref.dtype)
        products = mixed * q_ref[pl.ds(base, STEP)].astype(jnp.float32)
        part_acc[...] += jnp.sum(products.reshape(STEP // 8, 8, width), axis=0)
        return carry

    lax.fori_loop(0, groups, grad_step, 0, unroll=True)

    part_rows[0] = jnp.sum(part_acc[...], axis=0, keepdims=True)

    def part_copy(source, slot, target):
        return send(source, part_in.at[slot], part_send.at[slot], part_recv.at[slot], {"ctx": target})

    x_peers = [(peer + along) % n_ctx for peer in y_peers]
    targets = x_peers + y_peers + [far_x]
    spread = [part_copy(part_rows.at[0], at, target) for at, target in enumerate(targets)]
    on_up = part_copy(part_rows.at[1], 9, y_peers[0])
    on_down = part_copy(part_rows.at[2], 10, y_peers[1])
    pl.semaphore_wait(met.at[3], 1)
    for copy in spread:
        copy.start()
    key_grads()
    spread[2].wait_recv()
    spread[6].wait_recv()
    part_rows[1] = part_in[2] + part_in[6]
    on_up.start()
    for at in (1, 3, 5, 7):
        spread[at].wait_recv()
    part_rows[2] = part_in[1] + part_in[3] + part_in[5] + part_in[7]
    on_down.start()
    own_dk = dk_acc[pl.ds(HALO, tok)] * score_scale
    dk_acc[pl.ds(HALO, tok)] = own_dk
    dk_ref[...] = own_dk.astype(dk_ref.dtype)
    dv_ref[...] = dv_acc[pl.ds(HALO, tok)].astype(dv_ref.dtype)
    for at in (0, 4, 8):
        spread[at].wait_recv()
    across = part_rows[0] + part_in[8] + part_rows[1] + part_rows[2] + part_in[0] + part_in[4]
    on_up.wait_recv()
    on_down.wait_recv()
    head_row[...] = across + part_in[9] + part_in[10]

    @pl.when(aside & ((row == half) | (row == half + 1)))
    def _():
        pl.semaphore_wait(here.at[0], 1)

    def head_copy(target, slot):
        return send(head_row, head_in.at[row], head_send.at[slot], head_recv.at[row], {"dp": target})

    for other in range(HEADS):
        owner = HEADS * mine + other

        @pl.when(owner != d)
        def _():
            head_copy(owner, other).start()

        @pl.when(owner == d)
        def _():
            head_in[row] = head_row[...]

    @pl.when(c > 0)
    def _():
        back_dk.start()

    @pl.when(c < n_ctx - 1)
    def _():
        back_dv.wait_recv()

    @pl.when(c < n_ctx - 1)
    def _():
        dv_ref[pl.ds(tok - HALO, HALO)] = (
            dv_acc[pl.ds(tok, HALO)] + dv_in[...].astype(jnp.float32)
        ).astype(dv_ref.dtype)
        back_dk.wait_recv()
        dk_ref[pl.ds(tok - HALO, HALO)] = (
            dk_acc[pl.ds(tok, HALO)] + dk_in[...].astype(jnp.float32)
        ).astype(dk_ref.dtype)

    for other in range(HEADS):
        user = row + HEADS * other

        @pl.when(user != d)
        def _():
            send(
                head_row, head_in.at[other], head_send.at[0], head_recv.at[other], {"dp": user}
            ).wait_recv()

    whole = head_in[0]
    for other in range(1, HEADS):
        whole = whole + head_in[other]
    whole = pltpu.roll(jnp.broadcast_to(whole, (8, width)), (width - 16 * mine) % width, 1)
    gg_ref[...] = whole[0:1, 0 : gg_ref.shape[1]]

    for other in range(HEADS):
        owner = HEADS * mine + other

        @pl.when(owner != d)
        def _():
            head_copy(owner, other).wait_send()

    for copy in [*spread, on_up, on_down]:
        copy.wait_send()

    @pl.when(jnp.logical_not(diagonal))
    def _():
        to_root.wait_send()

    for t in range(HEADS):

        @pl.when(sends[t])
        def _():
            feed(t).wait_send()

    @pl.when(hands_over)
    def _():
        over.wait_send()

    @pl.when(c < n_ctx - 1)
    def _():
        for piece in range(4):
            halo_copy(0, piece, k_hbm, k_ext).wait_send()
            halo_copy(1, piece, v_hbm, v_ext).wait_send()

    @pl.when(c > 0)
    def _():
        back_dv.wait_send()
        back_dk.wait_send()


def deliver(*refs):
    sources, targets, held, sems = refs[:4], refs[4:8], refs[8:12], refs[12]
    loads = [
        pltpu.make_async_copy(source, hold, sems.at[0, at])
        for at, (source, hold) in enumerate(zip(sources, held))
    ]
    stores = [
        pltpu.make_async_copy(hold, target, sems.at[1, at])
        for at, (target, hold) in enumerate(zip(targets, held))
    ]
    for load in loads:
        load.start()
    for load, store in zip(loads, stores):
        load.wait()
        store.start()
    for store in stores:
        store.wait()


def on_device(queries, keys, values, grad_out, gain, doc_start, win_start):
    _, tok, width = queries.shape
    n_ctx = lax.axis_size("ctx")
    seqs = doc_start.shape[0]
    share = gain.shape[0]
    window = STEP + HALO
    groups = tok // STEP
    wide = (HALO + tok, width)
    hbm = pl.BlockSpec(memory_space=pl.ANY)
    vmem = pl.BlockSpec(memory_space=pltpu.VMEM)
    dma = pltpu.SemaphoreType.DMA


    grads = pl.pallas_call(
        functools.partial(body, n_ctx),
        out_shape=[jax.ShapeDtypeStruct((tok, width), jnp.bfloat16)] * 3
        + [jax.ShapeDtypeStruct((1, share), jnp.float32)],
        in_specs=[hbm] * 4 + [vmem] + [hbm] * 2,
        out_specs=[vmem] * 4,
        scratch_shapes=[
            pltpu.VMEM((tok, width), jnp.bfloat16),
            pltpu.VMEM((tok, width), jnp.bfloat16),
            pltpu.VMEM(wide, jnp.bfloat16),
            pltpu.VMEM(wide, jnp.bfloat16),
            pltpu.VMEM((width, HALO + tok), jnp.bfloat16),
            pltpu.VMEM((tok, width), jnp.bfloat16),
            pltpu.VMEM((seqs, tok), jnp.int32),
            pltpu.VMEM((seqs, tok), jnp.int32),
            pltpu.VMEM((seqs, tok), jnp.int32),
            pltpu.VMEM((window, STEP), jnp.float32),
            pltpu.VMEM((groups, window, STEP), jnp.bfloat16),
            pltpu.VMEM((groups, window, STEP), jnp.float32),
            pltpu.VMEM((groups, window, STEP), jnp.bfloat16),
            pltpu.VMEM(wide, jnp.float32),
            pltpu.VMEM(wide, jnp.float32),
            pltpu.VMEM((HALO, width), jnp.bfloat16),
            pltpu.VMEM((HALO, width), jnp.bfloat16),
            pltpu.VMEM((HALO, width), jnp.bfloat16),
            pltpu.VMEM((HALO, width), jnp.bfloat16),
            pltpu.VMEM((1, width), jnp.float32),
            pltpu.VMEM((1, width), jnp.float32),
            pltpu.VMEM((HEADS, 1, width), jnp.float32),
            pltpu.VMEM((1, width), jnp.float32),
            pltpu.VMEM((3, 1, width), jnp.float32),
            pltpu.VMEM((11, 1, width), jnp.float32),
            pltpu.VMEM((1, width), jnp.float32),
            pltpu.VMEM((HEADS, 1, width), jnp.float32),
            pltpu.VMEM((8, width), jnp.float32),
            dma((6,)),
            dma((2, 4)),
            dma((2, 4)),
            dma((2,)),
            dma((2,)),
            dma((1,)),
            dma((HEADS,)),
            dma((HEADS,)),
            dma((1,)),
            dma((11,)),
            dma((11,)),
            dma((HEADS,)),
            dma((HEADS,)),
            pltpu.SemaphoreType.REGULAR((4,)),
            pltpu.SemaphoreType.REGULAR((HEADS,)),
            pltpu.SemaphoreType.REGULAR((1,)),
        ],
        compiler_params=pltpu.CompilerParams(
            collective_id=0, has_side_effects=True, vmem_limit_bytes=60 << 20
        ),
    )(
        queries.reshape(tok, width),
        keys.reshape(tok, width),
        values.reshape(tok, width),
        grad_out.reshape(tok, width),
        gain.reshape(1, share),
        doc_start,
        win_start,
    )
    grads = pl.pallas_call(
        deliver,
        out_shape=[jax.ShapeDtypeStruct(grad.shape, grad.dtype) for grad in grads],
        in_specs=[hbm] * 4,
        out_specs=[hbm] * 4,
        scratch_shapes=[pltpu.VMEM(grad.shape, grad.dtype) for grad in grads] + [dma((2, 4))],
        compiler_params=pltpu.CompilerParams(vmem_limit_bytes=60 << 20),
    )(*grads)
    shape = (1, tok, width)
    return (
        grads[0].reshape(shape),
        grads[1].reshape(shape),
        grads[2].reshape(shape),
        grads[3].reshape(share),
    )


def solution(mesh):
    rows = P("dp", "ctx", None)
    return jax.shard_map(
        on_device,
        mesh=mesh,
        in_specs=(rows, rows, rows, rows, P("dp"), P(), P()),
        out_specs=(rows, rows, rows, P("dp")),
        check_vma=False,
    )
```
